512 devices in a mesh: ctx: 128 (over y, z, x_hi), tp: 4 (over x_lo, core).
Axes of the slice: x: 4 (x_hi: 2, x_lo: 2; x = x_hi * 2 + x_lo), y: 8, z: 8, core: 2. Of those that a mesh axis runs over, the one named last changes fastest.
Arguments:
- q_input: bfloat16 [16384, 4096], P('ctx', 'tp'), may hold values from -6 to 6
- k_input: bfloat16 [16384, 4096], P('ctx', 'tp'), may hold values from -6 to 6
- v_input: bfloat16 [16384, 4096], P('ctx', 'tp'), may hold values from -6 to 6
- resid: bfloat16 [16384, 4096], P('ctx', 'tp'), may hold values from -18 to 18
- lengths: int32 [8], replicated, may hold values from 1 to 8192, 16384 in all
- short_filter: bfloat16 [3, 256, 7], P(None, 'tp'), may hold values from -2 to 2
- long_filter: bfloat16 [256, 128], P('tp'), may hold values from -0.5 to 0.5
- skip: float32 [4096], P('tp'), may hold values from -1 to 1
- gain: float32 [4096], P('tp'), may hold values from 0.1 to 1.9
- cotangent: bfloat16 [16384, 4096], P('ctx', 'tp'), may hold values from -12 to 12
Outputs:
- normed: bfloat16 [16384, 4096], P('ctx', 'tp')
- grad_q: bfloat16 [16384, 4096], P('ctx', 'tp')
- grad_k: bfloat16 [16384, 4096], P('ctx', 'tp')
- grad_v: bfloat16 [16384, 4096], P('ctx', 'tp')
- grad_short: float32 [3, 256, 7], P(None, 'tp')
- grad_long: float32 [256, 128], P('tp')
- grad_skip: float32 [4096], P('tp')
- grad_gain: float32 [4096], P('tp')
The draws below stay inside these ranges and needn't reach their ends.
All inputs are finite; a program needn't handle non-finite values.
Results may differ from the reference program's by a relative error of at most 0.0047.
The reference program's roundings to bfloat16 on the way (of `gated`) count: a program that leaves them out, or rounds other values in their place, can miss the bound.
Values may be sent and summed in bfloat16 or wider, within the bound.
A program may use at most 128 MiB of HBM per device.

```python
import math
import jax
import jax.numpy as jnp
import numpy as np
from jax import lax

C = 4096
GS = 16
K = 128
KS = 7
GROUPS = 256
TOKENS = 16384
NSEQ = 8
SEQ_MOST = 8192


def draw_resid(key, part):
    first, second = jax.random.split(key)
    ramp = jnp.power(3.0, jnp.arange(C, dtype=jnp.float32) / C)
    column = ramp * jnp.exp(jax.random.uniform(second, (C,), jnp.float32) * math.log(10.0))
    base = jax.random.truncated_normal(first, -4.0, 4.0, (TOKENS, C), jnp.float32)
    return (0.15 * base * column[None, :]).astype(jnp.bfloat16)


def draw_cotangent(key, part):
    first = jax.random.fold_in(key, 0)
    ramp = jnp.power(3.0, jnp.arange(TOKENS, dtype=jnp.float32) / TOKENS)
    base = jax.random.truncated_normal(first, -4.0, 4.0, (TOKENS, C), jnp.float32)
    values = base * ramp[:, None]
    return values.astype(jnp.bfloat16)


def shard_levels(stream_key, dims, shards, smallest, largest):
    level, own = 1.0, jax.random.fold_in(stream_key, 6)
    for axis_at, blocks in shards:
        draws = jnp.exp(jax.random.uniform(jax.random.fold_in(own, axis_at), (blocks,), jnp.float32, smallest / len(shards), largest / len(shards)))
        level = level * jnp.repeat(draws, dims[axis_at] // blocks).reshape([-1 if axis == axis_at else 1 for axis in range(len(dims))])
    return level


def length_profile(count, total, limit, lean):
    portions = [(1 << 20) // math.isqrt(grade ** lean) + 1 for grade in range(2, count + 1)]
    surplus, given = total - limit - (count - 1), [1] * (count - 1)
    while surplus > 0:
        free = [i for i in range(count - 1) if given[i] < limit]
        whole, left = sum([portions[i] for i in free]), surplus
        for i in free:
            more = min(limit - given[i], max(1, left * portions[i] // whole), surplus)
            given[i] = given[i] + more
            surplus = surplus - more
    return np.array([limit] + given)


def uneven_parts(own_key, number_of, total, limit, slope):
    if number_of == 2:
        one = jax.random.randint(own_key, (), max(1, total - limit), min(limit, total - 1) + 1)
        return jnp.stack([one, total - one])
    sizes = jnp.asarray(length_profile(number_of, total, limit, slope), jnp.int32)
    couples = (number_of - 1) // 2
    donor, taker = sizes[1:1 + 2 * couples:2], sizes[2:2 + 2 * couples:2]
    slack = jnp.minimum(donor - 1, limit - taker)
    moved = jax.random.randint(jax.random.fold_in(own_key, 1), (couples,), 0, 1 << 20) % (slack + 1)
    sizes = sizes.at[1:1 + 2 * couples:2].set(donor - moved).at[2:2 + 2 * couples:2].set(taker + moved)
    return sizes[jax.random.permutation(jax.random.fold_in(own_key, 2), number_of)]


def noise(own_key, shape, scale, bound, pieces=(), kind=jnp.bfloat16):
    level = shard_levels(own_key, shape, pieces, -0.22, 0.18) if pieces else 1.0
    drawn = jax.random.normal(own_key, shape, jnp.float32) * scale * level
    return jnp.minimum(jnp.maximum(drawn, -bound), bound).astype(kind)


def setup_inputs(seed: int = 0) -> dict:
    seeds = jax.random.split(jax.random.key(seed), 11)
    q_input = noise(seeds[0], (TOKENS, C), 1.0, 6.0, ((0, 128), (1, 4)))
    k_input = noise(seeds[1], (TOKENS, C), 1.0, 6.0, ((0, 128), (1, 4)))
    v_input = noise(seeds[2], (TOKENS, C), 1.0, 6.0, ((0, 128), (1, 4)))
    resid = draw_resid(jax.random.fold_in(seeds[10], 71), 0)
    lengths = uneven_parts(seeds[4], NSEQ, TOKENS, SEQ_MOST, 2).astype(jnp.int32)
    short_filter = noise(seeds[5], (3, GROUPS, KS), KS ** -0.5, 2.0, ((1, 4),))
    long_filter = noise(seeds[6], (GROUPS, K), K ** -0.5, 0.5, ((0, 4),))
    skip = jnp.clip(jax.random.uniform(seeds[7], (C,), jnp.float32, -1.0, 1.0) * shard_levels(seeds[7], (C,), ((0, 4),), -0.4, 0.0), -1.0, 1.0)
    gain = jnp.clip(1.0 + 0.18 * jax.random.normal(seeds[8], (C,), jnp.float32), 0.1, 1.9)
    cotangent = draw_cotangent(jax.random.fold_in(seeds[10], 71), 0)
    return {"q_input": q_input, "k_input": k_input, "v_input": v_input, "resid": resid, "lengths": lengths, "short_filter": short_filter, "long_filter": long_filter, "skip": skip, "gain": gain, "cotangent": cotangent}


EPS = 1e-06
HIGH = lax.Precision.HIGHEST

def positions(lengths, row_ids):
    finish = jnp.cumsum(lengths).astype(jnp.int32)
    starts = finish - lengths
    before = starts[None, :] <= row_ids[:, None]
    begins = lax.optimization_barrier(jnp.max(jnp.where(before, starts[None, :], jnp.zeros_like(starts)[None, :]), axis=1))
    return (row_ids - begins).astype(jnp.int32)

def toeplitz(filters):
    groups, width = filters.shape
    reverse = filters[:, ::-1]
    banded = jnp.broadcast_to(reverse[:, None, :], (groups, width, width))
    banded = jnp.concatenate([banded, jnp.zeros((groups, width, width + 1), filters.dtype)], axis=2)
    flattened = banded.reshape(groups, width * (2 * width + 1))
    flattened = jnp.concatenate([jnp.zeros((groups, 1), filters.dtype), flattened], axis=1)[:, :2 * width * width]
    return flattened.reshape(groups, width, 2 * width)

def diagonals(square):
    groups, width, span = square.shape
    flattened = square.reshape(groups, width * span)
    flattened = jnp.concatenate([flattened[:, 1:], jnp.zeros((groups, width + 1), square.dtype)], axis=1)
    skewed = flattened.reshape(groups, width, span + 1)[:, :, :width]
    return skewed[:, :, ::-1]

def window_mask(row_pos, width):
    lag = jnp.arange(width, dtype=jnp.int32)[:, None] + width - jnp.arange(2 * width, dtype=jnp.int32)[None, :]
    return row_pos[:, None] >= lag

def causal_short(values, weights, pos):
    length, channels = values.shape
    result = jnp.zeros((length, channels), jnp.float32)
    for j in range(KS):
        moved = jnp.concatenate([jnp.zeros((j, channels), values.dtype), values[:length - j]], axis=0)
        result = result + weights[:, j] * moved.astype(jnp.float32) * (pos >= j)[:, None]
    return result

def anticausal_short(grads, weights, pos):
    length, channels = grads.shape
    result = jnp.zeros((length, channels), jnp.float32)
    for j in range(KS):
        masked = grads.astype(jnp.float32) * (pos >= j)[:, None]
        moved = jnp.concatenate([masked[j:], jnp.zeros((j, channels), jnp.float32)], axis=0)
        result = result + weights[:, j] * moved
    return result

def short_grads(grads, values, pos):
    length, channels = values.shape
    columns = []
    for j in range(KS):
        moved = jnp.concatenate([jnp.zeros((j, channels), values.dtype), values[:length - j]], axis=0)
        columns.append(lax.optimization_barrier(jnp.sum(grads.astype(jnp.float32) * moved.astype(jnp.float32) * (pos >= j)[:, None], axis=0)))
    return jnp.stack(columns, axis=1)

def long_forward(gated_groups, matrix, pos):
    groups, members, length = gated_groups.shape
    width = matrix.shape[1]
    padded = jnp.concatenate([jnp.zeros((groups, members, width), gated_groups.dtype), gated_groups], axis=2)

    def one_block(b):
        begin = b * width
        source = lax.dynamic_slice_in_dim(padded, begin, 2 * width, axis=2)
        row_pos = lax.dynamic_slice_in_dim(pos, begin, width)
        masked = matrix * window_mask(row_pos, width).astype(matrix.dtype)[None]
        return jnp.einsum('gcs,gts->gct', source.astype(jnp.float32), masked.astype(jnp.float32), precision=HIGH)
    outs = lax.map(one_block, jnp.arange(length // width, dtype=jnp.int32))
    return jnp.transpose(outs, (1, 2, 0, 3)).reshape(groups, members, length)

def long_backward(grad_groups, gated_groups, matrix, pos):
    groups, members, length = gated_groups.shape
    width = matrix.shape[1]
    padded = jnp.concatenate([jnp.zeros((groups, members, width), gated_groups.dtype), gated_groups], axis=2)

    def step(b, carry):
        accum, filt_grad = carry
        begin = jnp.asarray(b, jnp.int32) * width
        source = lax.dynamic_slice_in_dim(padded, begin, 2 * width, axis=2).astype(jnp.float32)
        row_pos = lax.dynamic_slice_in_dim(pos, begin, width)
        mask_bool = window_mask(row_pos, width)
        masked = (matrix * mask_bool.astype(matrix.dtype)[None]).astype(jnp.float32)
        block_grad = lax.dynamic_slice_in_dim(grad_groups, begin, width, axis=2).astype(jnp.float32)
        contrib = jnp.einsum('gct,gts->gcs', block_grad, masked, precision=HIGH)
        current = lax.dynamic_slice_in_dim(accum, begin, 2 * width, axis=2)
        accum = lax.dynamic_update_slice_in_dim(accum, current + contrib, begin, axis=2)
        cross = jnp.einsum('gct,gcs->gts', block_grad, source, precision=HIGH) * mask_bool.astype(jnp.float32)[None]
        filt_grad = filt_grad + lax.optimization_barrier(jnp.sum(diagonals(cross), axis=1))
        return (accum, filt_grad)
    start_acc = jnp.zeros((groups, members, length + width), jnp.float32)
    start_grad = jnp.zeros((groups, width), jnp.float32)
    accum, filt_grad = lax.fori_loop(0, length // width, step, (start_acc, start_grad))
    return (accum[:, :, width:], filt_grad)

def reference(q_input, k_input, v_input, resid, lengths, short_filter, long_filter, skip, gain, cotangent):
    block_width = math.gcd(C, 512)
    block_count = C // block_width
    block_groups = block_width // GS
    pos = positions(lengths, jnp.arange(TOKENS, dtype=jnp.int32))

    def split(array):
        return jnp.transpose(array.reshape(TOKENS, block_count, block_width), (1, 0, 2))

    def merge(array):
        return jnp.transpose(array, (1, 0, 2)).reshape(TOKENS, C)
    short_blocks = jnp.transpose(short_filter.reshape(3, block_count, block_groups, KS), (1, 0, 2, 3))
    long_blocks = long_filter.reshape(block_count, block_groups, K)
    skip_blocks = skip.reshape(block_count, block_width)
    gain_blocks = gain.reshape(block_count, block_width)

    def expand(taps):
        wide = jnp.broadcast_to(taps.astype(jnp.float32)[:, :, None, :], (3, block_groups, GS, KS))
        return wide.reshape(3, block_width, KS)

    def to_groups(array):
        return array.T.reshape(block_groups, GS, TOKENS)

    def from_groups(array):
        return array.reshape(block_width, TOKENS).T

    def forward(q_blk, k_blk, v_blk, taps, long_taps, skip_blk):
        table = expand(taps)
        q_short = causal_short(q_blk, table[0], pos)
        k_short = causal_short(k_blk, table[1], pos)
        v_short = causal_short(v_blk, table[2], pos)
        gated = (k_short * v_short).astype(jnp.bfloat16)
        matrix = toeplitz(long_taps)
        conv = from_groups(long_forward(to_groups(gated), matrix, pos))
        mixed = conv + skip_blk[None, :] * gated.astype(jnp.float32)
        return (table, q_short, k_short, v_short, gated, matrix, mixed)

    def first_pass(items):
        q_blk, k_blk, v_blk, x_blk, taps, long_taps, skip_blk = items
        outs = forward(q_blk, k_blk, v_blk, taps, long_taps, skip_blk)
        return x_blk.astype(jnp.float32) + outs[1] * outs[6]
    summed = lax.map(first_pass, (split(q_input), split(k_input), split(v_input), split(resid), short_blocks, long_blocks, skip_blocks))
    cot_blocks = split(cotangent)
    squares = lax.optimization_barrier(jnp.sum(summed * summed, axis=(0, 2)))
    inverse = lax.rsqrt(squares / C + EPS)
    mean_mix = lax.optimization_barrier(jnp.sum(gain_blocks[:, None, :] * cot_blocks.astype(jnp.float32) * summed, axis=(0, 2))) / C

    def second_pass(items):
        q_blk, k_blk, v_blk, cot_blk, sum_blk, taps, long_taps, skip_blk, gain_blk = items
        table, q_short, k_short, v_short, gated, matrix, mixed = forward(q_blk, k_blk, v_blk, taps, long_taps, skip_blk)
        normed = (gain_blk * sum_blk * inverse[:, None]).astype(jnp.bfloat16)
        scaled = gain_blk * cot_blk.astype(jnp.float32)
        grad_sum = inverse[:, None] * (scaled - sum_blk * (inverse * inverse * mean_mix)[:, None])
        grad_mixed = (grad_sum * q_short).astype(jnp.bfloat16)
        grad_qs = (grad_sum * mixed).astype(jnp.bfloat16)
        grad_gain = lax.optimization_barrier(jnp.sum(cot_blk.astype(jnp.float32) * sum_blk * inverse[:, None], axis=0))
        grad_conv, grad_long = long_backward(to_groups(grad_mixed), to_groups(gated), matrix, pos)
        grad_gated = skip_blk * grad_mixed.astype(jnp.float32) + from_groups(grad_conv)
        grad_skip = lax.optimization_barrier(jnp.sum(grad_mixed.astype(jnp.float32) * gated.astype(jnp.float32), axis=0))
        grad_ks = (grad_gated * v_short).astype(jnp.bfloat16)
        grad_vs = (grad_gated * k_short).astype(jnp.bfloat16)
        grad_q = anticausal_short(grad_qs, table[0], pos).astype(jnp.bfloat16)
        grad_k = anticausal_short(grad_ks, table[1], pos).astype(jnp.bfloat16)
        grad_v = anticausal_short(grad_vs, table[2], pos).astype(jnp.bfloat16)
        per_channel = jnp.stack([short_grads(grad_qs, q_blk, pos), short_grads(grad_ks, k_blk, pos), short_grads(grad_vs, v_blk, pos)], axis=0)
        grad_short = lax.optimization_barrier(jnp.sum(per_channel.reshape(3, block_groups, GS, KS), axis=2))
        return (normed, grad_q, grad_k, grad_v, grad_short, grad_long, grad_skip, grad_gain)
    results = lax.map(second_pass, (split(q_input), split(k_input), split(v_input), cot_blocks, summed, short_blocks, long_blocks, skip_blocks, gain_blocks))
    grad_short = jnp.transpose(results[4], (1, 0, 2, 3)).reshape(3, GROUPS, KS)
    return (merge(results[0]), merge(results[1]), merge(results[2]), merge(results[3]), grad_short, results[5].reshape(GROUPS, K), results[6].reshape(C), results[7].reshape(C))
```

```python
import functools

import jax
import jax.numpy as jnp
from jax import lax
from jax.experimental import pallas as pl
from jax.experimental.pallas import tpu as pltpu
from jax.sharding import PartitionSpec as P

C = 4096
GS = 16
K = 128
KS = 7


EPS = 1e-06
MESH_ID = pl.DeviceIdType.MESH
INNER = 16


def reduce_kernel(count, x_ref, o_ref, first, second, s1, r1, s2, r2, s3, r3):
    me = lax.axis_index("ctx")
    outer = count // INNER
    hi = me // INNER
    lo = me % INNER

    def inner_peer(k):
        return (lo + k) % INNER

    def outer_peer(k):
        return (hi + k) % outer

    barrier = pltpu.get_barrier_semaphore()
    for k in range(1, INNER):
        pl.semaphore_signal(
            barrier, inc=1, device_id={"ctx": hi * INNER + inner_peer(k)}, device_id_type=MESH_ID
        )
    for k in range(1, outer):
        pl.semaphore_signal(
            barrier, inc=1, device_id={"ctx": outer_peer(k) * INNER + lo}, device_id_type=MESH_ID
        )
    pl.semaphore_wait(barrier, INNER + outer - 2)

    def scatter(k):
        peer = inner_peer(k)
        return pltpu.make_async_remote_copy(
            src_ref=x_ref.at[peer],
            dst_ref=first.at[lo],
            send_sem=s1.at[k],
            recv_sem=r1.at[lo],
            device_id={"ctx": hi * INNER + peer},
            device_id_type=MESH_ID,
        )

    def exchange(k):
        return pltpu.make_async_remote_copy(
            src_ref=second.at[hi],
            dst_ref=second.at[hi],
            send_sem=s2.at[k],
            recv_sem=r2.at[hi],
            device_id={"ctx": outer_peer(k) * INNER + lo},
            device_id_type=MESH_ID,
        )

    def gather(k):
        return pltpu.make_async_remote_copy(
            src_ref=o_ref.at[lo],
            dst_ref=o_ref.at[lo],
            send_sem=s3.at[k],
            recv_sem=r3.at[lo],
            device_id={"ctx": hi * INNER + inner_peer(k)},
            device_id_type=MESH_ID,
        )

    def arrived(sem, buf, slot):
        pltpu.make_async_copy(buf.at[slot], buf.at[slot], sem.at[slot]).wait()

    for k in range(1, INNER):
        scatter(k).start()
    total = x_ref[lo]
    for k in range(1, INNER):
        slot = inner_peer(INNER - k)
        arrived(r1, first, slot)
        total = total + first[slot]
    second[hi] = total
    for k in range(1, outer):
        exchange(k).start()
    for k in range(1, outer):
        arrived(r2, second, outer_peer(outer - k))
    total = second[0]
    for i in range(1, outer):
        total = total + second[i]
    o_ref[lo] = total
    for k in range(1, INNER):
        gather(k).start()
    for k in range(1, INNER):
        arrived(r3, o_ref, inner_peer(INNER - k))
    for k in range(1, INNER):
        scatter(k).wait_send()
        gather(k).wait_send()
    for k in range(1, outer):
        exchange(k).wait_send()


def reduced(x):
    count = lax.axis_size("ctx")
    outer = count // INNER
    return pl.pallas_call(
        functools.partial(reduce_kernel, count),
        out_shape=jax.ShapeDtypeStruct(x.shape, jnp.float32),
        in_specs=[pl.BlockSpec(memory_space=pltpu.VMEM)],
        out_specs=pl.BlockSpec(memory_space=pltpu.VMEM),
        scratch_shapes=[
            pltpu.VMEM(x.shape, jnp.float32),
            pltpu.VMEM((outer,) + x.shape[1:], jnp.float32),
            pltpu.SemaphoreType.DMA((INNER,)),
            pltpu.SemaphoreType.DMA((INNER,)),
            pltpu.SemaphoreType.DMA((outer,)),
            pltpu.SemaphoreType.DMA((outer,)),
            pltpu.SemaphoreType.DMA((INNER,)),
            pltpu.SemaphoreType.DMA((INNER,)),
        ],
        compiler_params=pltpu.CompilerParams(collective_id=0, has_side_effects=True),
        name="grad_reduce",
    )(x)


def shifted(x, axis, by):
    count = lax.axis_size(axis)
    pairs = [(i, i + by) for i in range(count) if 0 <= i + by < count]
    return lax.ppermute(x, axis, pairs)


def positions(lengths, row_ids):
    finish = jnp.cumsum(lengths)
    starts = finish - lengths
    before = starts[None, :] <= row_ids[:, None]
    begins = jnp.max(jnp.where(before, starts[None, :], jnp.zeros_like(starts)[None, :]), axis=1)
    return row_ids - begins


def toeplitz(filters):
    groups, width = filters.shape
    reverse = filters[:, ::-1]
    banded = jnp.broadcast_to(reverse[:, None, :], (groups, width, width))
    banded = jnp.concatenate([banded, jnp.zeros((groups, width, width + 1), filters.dtype)], axis=2)
    flattened = banded.reshape(groups, width * (2 * width + 1))
    flattened = jnp.concatenate([jnp.zeros((groups, 1), filters.dtype), flattened], axis=1)[
        :, : 2 * width * width
    ]
    return flattened.reshape(groups, width, 2 * width)


def diagonals(square):
    groups, width, span = square.shape
    flattened = square.reshape(groups, width * span)
    flattened = jnp.concatenate(
        [flattened[:, 1:], jnp.zeros((groups, width + 1), square.dtype)], axis=1
    )
    skewed = flattened.reshape(groups, width, span + 1)[:, :, :width]
    return skewed[:, :, ::-1]


def window_mask(row_pos, width):
    lag = (
        jnp.arange(width, dtype=jnp.int32)[:, None]
        + width
        - jnp.arange(2 * width, dtype=jnp.int32)[None, :]
    )
    return row_pos[:, None] >= lag


def causal_sum(extended, weights, pos, length):
    lead = extended.shape[0] - length
    result = jnp.zeros((length, extended.shape[1]), jnp.float32)
    for j in range(KS):
        moved = extended[lead - j : lead - j + length].astype(jnp.float32)
        result = result + weights[:, j] * moved * (pos >= j)[:, None]
    return result


def anticausal_sum(extended, weights, pos_after, length):
    result = jnp.zeros((length, extended.shape[1]), jnp.float32)
    for j in range(KS):
        moved = (
            extended[j : j + length].astype(jnp.float32) * (pos_after[j : j + length] >= j)[:, None]
        )
        result = result + weights[:, j] * moved
    return result


def tap_grads(grads, extended, pos, length):
    lead = extended.shape[0] - length
    columns = []
    for j in range(KS):
        moved = extended[lead - j : lead - j + length].astype(jnp.float32)
        columns.append(jnp.sum(grads.astype(jnp.float32) * moved * (pos >= j)[:, None], axis=0))
    return jnp.stack(columns, axis=1)


def to_groups(array, groups):
    return array.T.reshape(groups, GS, array.shape[0])


def from_groups(array):
    return array.reshape(-1, array.shape[2]).T


def shards(
    q_input, k_input, v_input, resid, lengths, short_filter, long_filter, skip, gain, cotangent
):
    length, channels = q_input.shape
    groups = channels // GS
    block_count = length // K
    first_row = lax.axis_index("ctx") * length
    pos_ext = positions(lengths, first_row + jnp.arange(length + K, dtype=jnp.int32))
    pos_local = pos_ext[:length]
    tap_table = jnp.broadcast_to(
        short_filter.astype(jnp.float32)[:, :, None, :], (3, groups, GS, KS)
    ).reshape(3, channels, KS)
    left_rims = shifted(
        (q_input[length - (KS - 1) :], k_input[length - (KS - 1) :], v_input[length - (KS - 1) :]),
        "ctx",
        1,
    )
    q_ext = jnp.concatenate([left_rims[0], q_input], axis=0)
    k_ext = jnp.concatenate([left_rims[1], k_input], axis=0)
    v_ext = jnp.concatenate([left_rims[2], v_input], axis=0)
    q_short = causal_sum(q_ext, tap_table[0], pos_local, length)
    k_short = causal_sum(k_ext, tap_table[1], pos_local, length)
    v_short = causal_sum(v_ext, tap_table[2], pos_local, length)
    gated = (k_short * v_short).astype(jnp.bfloat16)
    matrix = toeplitz(long_filter)
    masks = [window_mask(pos_ext[b * K : (b + 1) * K], K) for b in range(block_count + 1)]
    matrices = [matrix * mask_bool.astype(jnp.bfloat16)[None] for mask_bool in masks]
    lag_range = jnp.arange(K, dtype=jnp.int32)
    lag_masks = [
        (pos_ext[b * K : (b + 1) * K][:, None] >= lag_range[None, :]).astype(jnp.float32)
        for b in range(block_count + 1)
    ]
    gated_groups = to_groups(gated, groups)
    zero_block = jnp.zeros((groups, GS, K), jnp.bfloat16)
    gated_padded = jnp.concatenate([zero_block, gated_groups, zero_block], axis=2)
    pieces = [
        jnp.einsum(
            "gcs,gts->gct",
            gated_padded[:, :, b * K : b * K + 2 * K],
            matrices[b],
            preferred_element_type=jnp.float32,
        )
        for b in range(block_count + 1)
    ]
    arriving = shifted(pieces[block_count].reshape(channels, K), "ctx", 1)
    leading = pieces[0] + arriving.reshape(groups, GS, K)
    conv = jnp.concatenate([leading] + pieces[1:block_count], axis=2)
    mixed = from_groups(conv) + skip * gated.astype(jnp.float32)
    summed = resid.astype(jnp.float32) + q_short * mixed
    cot_float = cotangent.astype(jnp.float32)
    squares = jnp.sum(summed * summed, axis=1)
    products = jnp.sum(gain * cot_float * summed, axis=1)
    squares = lax.psum(squares, "tp")
    inverse = lax.rsqrt(squares / C + EPS)
    normed = (gain * summed * inverse[:, None]).astype(jnp.bfloat16)
    products = lax.psum(products, "tp")
    mean_mix = products / C
    scaled = gain * cot_float
    grad_sum = inverse[:, None] * (scaled - summed * (inverse * inverse * mean_mix)[:, None])
    grad_mixed = (grad_sum * q_short).astype(jnp.bfloat16)
    grad_qs = (grad_sum * mixed).astype(jnp.bfloat16)
    grad_gain = jnp.sum(cot_float * summed * inverse[:, None], axis=0)
    right_rims = shifted((grad_mixed[: K - 1], grad_qs[: KS - 1]), "ctx", -1)
    grad_rows = jnp.concatenate(
        [grad_mixed, right_rims[0], jnp.zeros((1, channels), jnp.bfloat16)], axis=0
    )
    grad_groups = to_groups(grad_rows, groups)
    accum = jnp.zeros((groups, GS, length + 2 * K), jnp.float32)
    grad_long = jnp.zeros((groups, K), jnp.float32)
    for b in range(block_count + 1):
        block_grad = grad_groups[:, :, b * K : (b + 1) * K]
        contrib = jnp.einsum(
            "gct,gts->gcs", block_grad, matrices[b], preferred_element_type=jnp.float32
        )
        accum = accum.at[:, :, b * K : b * K + 2 * K].add(contrib)
        cross = jnp.einsum(
            "gct,gcs->gts",
            block_grad,
            gated_padded[:, :, b * K : b * K + 2 * K],
            preferred_element_type=jnp.float32,
        )
        grad_long = grad_long + jnp.sum(diagonals(cross) * lag_masks[b][None], axis=1)
    grad_gated = skip * grad_mixed.astype(jnp.float32) + from_groups(accum[:, :, K : K + length])
    grad_skip = jnp.sum(grad_mixed.astype(jnp.float32) * gated.astype(jnp.float32), axis=0)
    grad_ks = (grad_gated * v_short).astype(jnp.bfloat16)
    grad_vs = (grad_gated * k_short).astype(jnp.bfloat16)
    gate_tails = shifted((grad_ks[: KS - 1], grad_vs[: KS - 1]), "ctx", -1)
    pos_after = pos_ext[: length + KS - 1]
    grad_q = anticausal_sum(
        jnp.concatenate([grad_qs, right_rims[1]], axis=0), tap_table[0], pos_after, length
    ).astype(jnp.bfloat16)
    grad_k = anticausal_sum(
        jnp.concatenate([grad_ks, gate_tails[0]], axis=0), tap_table[1], pos_after, length
    ).astype(jnp.bfloat16)
    grad_v = anticausal_sum(
        jnp.concatenate([grad_vs, gate_tails[1]], axis=0), tap_table[2], pos_after, length
    ).astype(jnp.bfloat16)
    per_channel = jnp.stack(
        [
            tap_grads(grad_qs, q_ext, pos_local, length),
            tap_grads(grad_ks, k_ext, pos_local, length),
            tap_grads(grad_vs, v_ext, pos_local, length),
        ],
        axis=0,
    )
    grad_short = jnp.sum(per_channel.reshape(3, groups, GS, KS), axis=2)
    parts = (grad_short, grad_long, grad_skip, grad_gain)
    sizes = [p.size for p in parts]
    flat = jnp.concatenate([p.reshape(-1) for p in parts])
    rows = INNER * 8
    flat = jnp.concatenate([flat, jnp.zeros((rows * 128 - flat.size,), jnp.float32)])
    flat = reduced(flat.reshape(INNER, 8, 128)).reshape(-1)
    totals = []
    at = 0
    for part, size in zip(parts, sizes):
        totals.append(flat[at : at + size].reshape(part.shape))
        at += size
    return (normed, grad_q, grad_k, grad_v, totals[0], totals[1], totals[2], totals[3])


def solution(mesh):
    placed = (
        P("ctx", "tp"),
        P("ctx", "tp"),
        P("ctx", "tp"),
        P("ctx", "tp"),
        P(),
        P(None, "tp", None),
        P("tp", None),
        P("tp"),
        P("tp"),
        P("ctx", "tp"),
    )
    return jax.shard_map(
        shards,
        mesh=mesh,
        in_specs=placed,
        out_specs=(
            P("ctx", "tp"),
            P("ctx", "tp"),
            P("ctx", "tp"),
            P("ctx", "tp"),
            P(None, "tp", None),
            P("tp", None),
            P("tp"),
            P("tp"),
        ),
        check_vma=False,
    )
```

```python
import functools

import jax
import jax.numpy as jnp
from jax import lax
from jax.experimental import pallas as pl
from jax.experimental.pallas import tpu as pltpu
from jax.sharding import PartitionSpec as P

C = 4096
GS = 16
K = 128
KS = 7
EPS = 1e-06
INNER = 16
MESH_ID = pl.DeviceIdType.MESH
F32 = jnp.float32
BF16 = jnp.bfloat16
HIGH = lax.Precision.HIGHEST
RIM = 8
HEAD = 16


def iota(shape, axis):
    return lax.broadcasted_iota(jnp.int32, shape, axis)


def skewed(x):
    return pltpu.roll(x, 0, 1, stride=1, stride_axis=0)


def body(
    count,
    tp_count,
    lengths,
    q_ref,
    k_ref,
    v_ref,
    resid_ref,
    cot_ref,
    short_ref,
    long_ref,
    skip_ref,
    gain_ref,
    normed_out,
    gq_out,
    gk_out,
    gv_out,
    gshort_out,
    glong_out,
    gskip_out,
    ggain_out,
    tail_s,
    tail_r,
    tail2_r,
    headk_r,
    headv_r,
    head_s,
    head_r,
    gext,
    gmx,
    gqs_s,
    gqs_r,
    xq,
    xk,
    xv,
    pk,
    pv,
    sq,
    sk,
    sv,
    mixed_s,
    summed_s,
    eq,
    ek,
    ev,
    fmat,
    umat,
    xmat,
    mats,
    xmasks,
    taps_m,
    prev_m,
    taps_w,
    wfwd,
    wrev,
    glong_s,
    tsum,
    stats,
    xs,
    first,
    second,
    result,
    hs,
    hr,
    ts,
    tr,
    s1,
    r1,
    s2,
    r2,
    s3,
    r3,
):
    length, width = q_ref.shape
    tiles = width // 128
    per = 128 // GS
    groups = width // GS
    ctx = lax.axis_index("ctx")
    tp = lax.axis_index("tp")
    outer = count // INNER
    hi = ctx // INNER
    lo = ctx % INNER
    total = count * length
    base = ctx * length

    def along(by):
        return (ctx + by + count) % count

    def inner_peer(k):
        return (lo + k) % INNER

    def outer_peer(k):
        return (hi + k) % outer

    def tp_peer(k):
        return (tp + k) % tp_count

    barrier = pltpu.get_barrier_semaphore()
    for by in (1, 2, -1, -2):
        pl.semaphore_signal(barrier, inc=1, device_id={"ctx": along(by)}, device_id_type=MESH_ID)
    for k in range(1, tp_count):
        pl.semaphore_signal(barrier, inc=1, device_id={"tp": tp_peer(k)}, device_id_type=MESH_ID)
    for k in range(1, INNER):
        pl.semaphore_signal(
            barrier, inc=1, device_id={"ctx": hi * INNER + inner_peer(k)}, device_id_type=MESH_ID
        )
    for k in range(1, outer):
        pl.semaphore_signal(
            barrier, inc=1, device_id={"ctx": outer_peer(k) * INNER + lo}, device_id_type=MESH_ID
        )

    def halo(slot, src, dst, by):
        return pltpu.make_async_remote_copy(
            src_ref=src,
            dst_ref=dst,
            send_sem=hs.at[slot],
            recv_sem=hr.at[slot],
            device_id={"ctx": along(by)},
            device_id_type=MESH_ID,
        )

    tails = halo(0, tail_s, tail_r, 1)
    tails2 = halo(1, tail_s.at[pl.ds(1, 2)], tail2_r, 2)
    heads_k = halo(2, k_ref.at[pl.ds(0, HEAD)], headk_r, 1)
    heads_v = halo(3, v_ref.at[pl.ds(0, HEAD)], headv_r, 1)
    heads_back = halo(4, head_s, head_r, -1)
    gated_copy = halo(5, gext.at[pl.ds(K + HEAD, K - HEAD)], gext.at[pl.ds(HEAD, K - HEAD)], 1)
    gm_copy = halo(6, gmx.at[pl.ds(0, K)], gmx.at[pl.ds(K, K)], -1)
    gm_far = halo(7, gmx.at[pl.ds(0, HEAD)], gmx.at[pl.ds(2 * K, HEAD)], -2)
    gqs_copy = halo(8, gqs_s, gqs_r, -1)

    for s, ref in enumerate((q_ref, k_ref, v_ref)):
        tail_s[s] = ref[length - HEAD :, :].astype(F32)[HEAD - RIM :].astype(BF16)
    head_s[0] = k_ref[0:HEAD, :].astype(F32)[:RIM].astype(BF16)
    head_s[1] = v_ref[0:HEAD, :].astype(F32)[:RIM].astype(BF16)

    pl.semaphore_wait(barrier, 4 + tp_count - 1 + INNER - 1 + outer - 1)
    tails.start()
    tails2.start()
    heads_k.start()
    heads_v.start()
    heads_back.start()

    starts = []
    at = jnp.int32(0)
    for i in range(lengths.shape[0]):
        starts.append(at)
        at = at + lengths[i]

    def position(token):
        begin = jnp.zeros_like(token)
        for start in starts:
            begin = jnp.where(token >= start, start, begin)
        return token - begin

    def flag(cond):
        return jnp.where(cond, 1.0, 0.0).astype(F32)

    token = base - RIM + iota((length + 2 * RIM, 128), 0)
    pos = position(token)
    for j in range(KS):
        taps_m[j] = flag((pos >= j) & (token < total))
    token = base - K + iota((HEAD, 128), 0)
    pos = position(token)
    for j in range(KS):
        prev_m[j] = flag(pos >= j)
    row = iota((K, 128), 0)
    col = iota((K, 128), 1)
    pos = position(base + row)
    mats[0] = flag((col > row) & (pos >= row - col + K))
    mats[1] = flag((col <= row) & (pos >= row - col))

    picks = flag(iota((groups, width), 1) // GS == iota((groups, width), 0)).astype(BF16)
    for s in range(3):
        table = lax.dot_general(
            short_ref[s], picks, (((0,), (0,)), ((), ())), preferred_element_type=F32
        )
        for t in range(tiles):
            taps_w[t, pl.ds(s * 8, KS), :] = table[:, t * 128 : (t + 1) * 128]

    def lanes(t):
        return pl.ds(pl.multiple_of(t * 128, 128), 128)

    def short_sum(buf, t, s, first_row, rows, mask, mask_row):
        result_sum = taps_w[t, pl.ds(s * 8, 1), :] * buf[t, pl.ds(RIM + first_row, rows), :]
        for j in range(1, KS):
            moved = buf[t, pl.ds(RIM + first_row - j, rows), :]
            result_sum = result_sum + taps_w[t, pl.ds(s * 8 + j, 1), :] * (
                moved * mask[j, pl.ds(mask_row, rows), :]
            )
        return result_sum

    rest = length - HEAD

    def gate_main(t, carry):
        xk[t, pl.ds(RIM, length), :] = k_ref[:, lanes(t)].astype(F32)
        xv[t, pl.ds(RIM, length), :] = v_ref[:, lanes(t)].astype(F32)
        ks = short_sum(xk, t, 1, HEAD, rest, taps_m, RIM + HEAD)
        vs = short_sum(xv, t, 2, HEAD, rest, taps_m, RIM + HEAD)
        sk[t, pl.ds(HEAD, rest), :] = ks
        sv[t, pl.ds(HEAD, rest), :] = vs
        gext[pl.ds(K + HEAD, rest), lanes(t)] = (ks * vs).astype(BF16)
        return carry

    lax.fori_loop(0, tiles, gate_main, 0)
    gated_copy.start()

    def query_main(t, carry):
        xq[t, pl.ds(RIM, length), :] = q_ref[:, lanes(t)].astype(F32)
        sq[t, pl.ds(HEAD, rest), :] = short_sum(xq, t, 0, HEAD, rest, taps_m, RIM + HEAD)
        return carry

    lax.fori_loop(0, tiles, query_main, 0)

    pos = position(base + col)
    mats[2] = flag((col >= row) & (pos >= col - row))
    token = base + K + col
    pos = position(token)
    mats[3] = flag((col < row) & (pos >= K + col - row) & (token < total))
    near_row = iota((8, 128), 0)
    near_col = iota((8, 128), 1)
    token = base + K + near_col
    pos = position(token)
    xmasks[0] = flag((near_col >= near_row) & (pos >= near_col - near_row) & (token < total))
    token = token + K
    pos = position(token)
    xmasks[1] = flag((near_col < near_row) & (pos >= K + near_col - near_row) & (token < total))

    flip = flag((row + col) % K == 0)
    wfwd[...] = long_ref[...].astype(F32)
    wrev[...] = jnp.dot(long_ref[...], flip.astype(BF16), preferred_element_type=F32)

    def build(t, carry):
        forward = wfwd[pl.ds(pl.multiple_of(t * per, per), per), :]
        backward = wrev[pl.ds(pl.multiple_of(t * per, per), per), :]
        extra = []
        for g in range(per):
            band = skewed(jnp.broadcast_to(backward[g : g + 1, :], (K, K)))
            fmat[t, pl.ds(g * K, K), pl.ds(0, K)] = (band * mats[0]).astype(BF16)
            fmat[t, pl.ds(g * K, K), pl.ds(K, K)] = (band * mats[1]).astype(BF16)
            band = skewed(jnp.broadcast_to(forward[g : g + 1, :], (K, K)))
            umat[t, pl.ds(g * K, K), pl.ds(0, K)] = (band * mats[2]).astype(BF16)
            umat[t, pl.ds(g * K, K), pl.ds(K, K)] = (band * mats[3]).astype(BF16)
            near = band[0:8, :]
            extra.append(jnp.concatenate([near * xmasks[0], near * xmasks[1]], axis=1))
        xmat[t] = jnp.concatenate(extra, axis=0).astype(BF16)
        return carry

    lax.fori_loop(0, tiles, build, 0)
    gmx[pl.ds(2 * K + HEAD, K - HEAD), :] = jnp.zeros((K - HEAD, width), BF16)

    tails.wait_recv()
    tails2.wait_recv()
    heads_k.wait_recv()
    heads_v.wait_recv()
    heads_back.wait_recv()
    for t in range(tiles):
        part = slice(t * 128, (t + 1) * 128)
        for s, buf in enumerate((xq, xk, xv)):
            buf[t, pl.ds(0, RIM), :] = tail_r[s, :, part].astype(F32)
        for s, (buf, prev, head) in enumerate(((xk, pk, headk_r), (xv, pv, headv_r))):
            buf[t, pl.ds(RIM + length, RIM), :] = head_r[s, :, part].astype(F32)
            prev[t, pl.ds(0, RIM), :] = tail2_r[s, :, part].astype(F32)
            prev[t, pl.ds(RIM, HEAD), :] = head[:, part].astype(F32)

    def gate_rims(t, carry):
        sq[t, pl.ds(0, HEAD), :] = short_sum(xq, t, 0, 0, HEAD, taps_m, RIM)
        ks = short_sum(xk, t, 1, 0, HEAD, taps_m, RIM)
        vs = short_sum(xv, t, 2, 0, HEAD, taps_m, RIM)
        sk[t, pl.ds(0, HEAD), :] = ks
        sv[t, pl.ds(0, HEAD), :] = vs
        gext[pl.ds(K, HEAD), lanes(t)] = (ks * vs).astype(BF16)
        sk[t, pl.ds(length, RIM), :] = short_sum(xk, t, 1, length, RIM, taps_m, RIM + length)
        sv[t, pl.ds(length, RIM), :] = short_sum(xv, t, 2, length, RIM, taps_m, RIM + length)
        ks = short_sum(pk, t, 1, 0, HEAD, prev_m, 0)
        vs = short_sum(pv, t, 2, 0, HEAD, prev_m, 0)
        gext[pl.ds(0, HEAD), lanes(t)] = (ks * vs).astype(BF16)
        return carry

    lax.fori_loop(0, tiles, gate_rims, 0)
    gated_copy.wait_recv()

    def select(products, rows):
        group = iota((rows, 128), 1) // GS
        picked = products[0:rows]
        for g in range(1, per):
            picked = jnp.where(group == g, products[g * rows : (g + 1) * rows], picked)
        return picked

    def mix(t, carry):
        squares, products = carry
        source = gext[:, lanes(t)]
        conv = select(jnp.dot(fmat[t], source, preferred_element_type=F32), K)
        gated = gext[pl.ds(K, K), lanes(t)].astype(F32)
        mixed = conv + skip_ref[:, lanes(t)] * gated
        summed = resid_ref[:, lanes(t)].astype(F32) + sq[t] * mixed
        mixed_s[t] = mixed
        summed_s[t] = summed
        squares = squares + summed * summed
        products = products + gain_ref[:, lanes(t)] * cot_ref[:, lanes(t)].astype(F32) * summed
        return squares, products

    zero = jnp.zeros((length, 128), F32)
    squares, products = lax.fori_loop(0, tiles, mix, (zero, zero))
    squares = jnp.sum(squares.T, axis=0, keepdims=True)
    products = jnp.sum(products.T, axis=0, keepdims=True)
    stats[tp] = jnp.where(near_row == 0, squares, products)

    def share(k):
        return pltpu.make_async_remote_copy(
            src_ref=stats.at[tp],
            dst_ref=stats.at[tp],
            send_sem=ts.at[k],
            recv_sem=tr.at[tp],
            device_id={"tp": tp_peer(k)},
            device_id_type=MESH_ID,
        )

    def arrived(sem, buf, slot):
        pltpu.make_async_copy(buf.at[slot], buf.at[slot], sem.at[slot]).wait()

    for k in range(1, tp_count):
        share(k).start()
    for k in range(1, tp_count):
        arrived(tr, stats, tp_peer(tp_count - k))
    both = stats[0]
    for i in range(1, tp_count):
        both = both + stats[i]
    both = both / (width * tp_count)
    shifted = both[0:1] + EPS
    inverse_row = lax.rsqrt(shifted)
    inverse_row = inverse_row * (1.5 - 0.5 * shifted * inverse_row * inverse_row)
    pull_row = inverse_row * inverse_row * both[1:2]
    inverse = jnp.broadcast_to(inverse_row, (128, length)).T
    pull = jnp.broadcast_to(pull_row, (128, length)).T
    mats[4] = inverse
    mats[5] = pull

    def grads(t, carry):
        inverse = mats[4]
        summed = summed_s[t]
        gain = gain_ref[:, lanes(t)]
        cot = cot_ref[:, lanes(t)].astype(F32)
        normed_out[:, lanes(t)] = (gain * summed * inverse).astype(BF16)
        grad_sum = inverse * (gain * cot - summed * mats[5])
        grad_mixed = (grad_sum * sq[t]).astype(BF16)
        gmx[pl.ds(0, K), lanes(t)] = grad_mixed
        grad_qs = (grad_sum * mixed_s[t]).astype(BF16)
        eq[t, pl.ds(0, length), :] = grad_qs.astype(F32)
        gqs_s[:, lanes(t)] = grad_qs.astype(F32)[:RIM].astype(BF16)
        gated = gext[pl.ds(K, K), lanes(t)].astype(F32)
        xs[8, pl.ds(t, 1), :] = jnp.sum(grad_mixed.astype(F32) * gated, axis=0, keepdims=True)
        xs[9, pl.ds(t, 1), :] = jnp.sum(cot * summed * inverse, axis=0, keepdims=True)
        return carry

    lax.fori_loop(0, tiles, grads, 0)
    gm_copy.start()
    gm_far.start()
    gqs_copy.start()

    def correlate(t, carry):
        grad_mixed = gmx[pl.ds(0, K), lanes(t)]
        source = gext[:, lanes(t)]
        group = iota((K, 128), 1) // GS
        left = jnp.concatenate(
            [jnp.where(group == g, grad_mixed, jnp.zeros_like(grad_mixed)) for g in range(per)], axis=0
        )
        cross = lax.dot_general(
            left, source, (((1,), (1,)), ((), ())), preferred_element_type=F32
        )
        for g in range(per):
            block = cross[g * K : (g + 1) * K]
            band = block[:, :K] * mats[0] + block[:, K:] * mats[1]
            folded = band[0:8]
            for a in range(1, K // 8):
                folded = folded + pltpu.roll(band[a * 8 : (a + 1) * 8], K - a * 8, 1)
            glong_s[pl.ds(pl.multiple_of(t * per * 8, 8) + g * 8, 8), :] = folded
        return carry

    lax.fori_loop(0, tiles, correlate, 0)
    folded = glong_s[pl.ds(0, groups, stride=8), :]
    for b in range(1, 8):
        folded = folded + pltpu.roll(glong_s[pl.ds(b, groups, stride=8), :], K - b, 1)
    turned = jnp.dot(folded, flip, precision=HIGH, preferred_element_type=F32)
    for t in range(tiles):
        xs[t] = turned[t * per : (t + 1) * per]
    tsum[...] = jnp.zeros_like(tsum)

    gm_copy.wait_recv()
    gm_far.wait_recv()
    gqs_copy.wait_recv()

    def back(t, carry):
        conv = select(
            jnp.dot(umat[t], gmx[pl.ds(0, 2 * K), lanes(t)], preferred_element_type=F32), K
        )
        extra = select(
            jnp.dot(xmat[t], gmx[pl.ds(K, 2 * K), lanes(t)], preferred_element_type=F32), 8
        )
        skip = skip_ref[:, lanes(t)]
        grad_gated = skip * gmx[pl.ds(0, K), lanes(t)].astype(F32) + conv
        ek[t, pl.ds(0, length), :] = (grad_gated * sv[t, pl.ds(0, length), :]).astype(BF16).astype(F32)
        ev[t, pl.ds(0, length), :] = (grad_gated * sk[t, pl.ds(0, length), :]).astype(BF16).astype(F32)
        near = gmx[pl.ds(K, HEAD), lanes(t)].astype(F32)[:RIM]
        grad_gated = skip * near + extra
        ek[t, pl.ds(length, RIM), :] = (grad_gated * sv[t, pl.ds(length, RIM), :]).astype(BF16).astype(F32)
        ev[t, pl.ds(length, RIM), :] = (grad_gated * sk[t, pl.ds(length, RIM), :]).astype(BF16).astype(F32)
        eq[t, pl.ds(length, RIM), :] = gqs_r[:, lanes(t)].astype(F32)
        for s, (buf, values, out) in enumerate(((eq, xq, gq_out), (ek, xk, gk_out), (ev, xv, gv_out))):
            own = values[t, pl.ds(RIM, length), :]
            result_sum = jnp.zeros((length, 128), F32)
            for j in range(KS):
                moved = buf[t, pl.ds(j, length), :] * taps_m[j, pl.ds(RIM + j, length), :]
                result_sum = result_sum + taps_w[t, pl.ds(s * 8 + j, 1), :] * moved
                tsum[t, pl.ds(s * 8 + j, 1), :] = jnp.sum(moved * own, axis=0, keepdims=True)
            out[:, lanes(t)] = result_sum.astype(BF16)
        return carry

    lax.fori_loop(0, tiles, back, 0)

    short_sums = jnp.zeros((24, 128), F32)
    for t in range(tiles):
        spread = flag(iota((128, 128), 0) // GS + t * per == iota((128, 128), 1))
        short_sums = short_sums + jnp.dot(
            tsum[t], spread, precision=HIGH, preferred_element_type=F32
        )
    for s in range(3):
        xs[10 + s] = short_sums[s * 8 : (s + 1) * 8]
    for i in range(13, INNER):
        xs[i] = jnp.zeros((8, 128), F32)

    def scatter(k):
        peer = inner_peer(k)
        return pltpu.make_async_remote_copy(
            src_ref=xs.at[peer],
            dst_ref=first.at[lo],
            send_sem=s1.at[k],
            recv_sem=r1.at[lo],
            device_id={"ctx": hi * INNER + peer},
            device_id_type=MESH_ID,
        )

    def exchange(k):
        return pltpu.make_async_remote_copy(
            src_ref=second.at[hi],
            dst_ref=second.at[hi],
            send_sem=s2.at[k],
            recv_sem=r2.at[hi],
            device_id={"ctx": outer_peer(k) * INNER + lo},
            device_id_type=MESH_ID,
        )

    def gather(k):
        return pltpu.make_async_remote_copy(
            src_ref=result.at[lo],
            dst_ref=result.at[lo],
            send_sem=s3.at[k],
            recv_sem=r3.at[lo],
            device_id={"ctx": hi * INNER + inner_peer(k)},
            device_id_type=MESH_ID,
        )

    for k in range(1, INNER):
        scatter(k).start()
    sums = xs[lo]
    for k in range(1, INNER):
        slot = inner_peer(INNER - k)
        arrived(r1, first, slot)
        sums = sums + first[slot]
    second[hi] = sums
    for k in range(1, outer):
        exchange(k).start()
    for k in range(1, outer):
        arrived(r2, second, outer_peer(outer - k))
    sums = second[0]
    for i in range(1, outer):
        sums = sums + second[i]
    result[lo] = sums
    for k in range(1, INNER):
        gather(k).start()

    for copy in (
        tails,
        tails2,
        heads_k,
        heads_v,
        heads_back,
        gated_copy,
        gm_copy,
        gm_far,
        gqs_copy,
    ):
        copy.wait_send()
    for k in range(1, tp_count):
        share(k).wait_send()
    for k in range(1, INNER):
        scatter(k).wait_send()
    for k in range(1, outer):
        exchange(k).wait_send()
    for k in range(1, INNER):
        arrived(r3, result, inner_peer(INNER - k))

    for t in range(tiles):
        glong_out[pl.ds(t * per, per), :] = result[t]
    gskip_out[...] = result[8]
    ggain_out[...] = result[9]
    for s in range(3):
        gshort_out[s] = result[10 + s].T[:groups, :KS]
    for k in range(1, INNER):
        gather(k).wait_send()


def shards(
    q_input, k_input, v_input, resid, lengths, short_filter, long_filter, skip, gain, cotangent
):
    length, width = q_input.shape
    tiles = width // 128
    groups = width // GS
    per = 128 // GS
    count = lax.axis_size("ctx")
    tp_count = lax.axis_size("tp")
    outer = count // INNER
    vmem = pl.BlockSpec(memory_space=pltpu.VMEM)
    large = jax.ShapeDtypeStruct((length, width), BF16)

    def tiled(rows):
        return pltpu.VMEM((tiles, rows, 128), F32)

    dma = pltpu.SemaphoreType.DMA
    outs = pl.pallas_call(
        functools.partial(body, count, tp_count),
        out_shape=(
            large,
            large,
            large,
            large,
            jax.ShapeDtypeStruct((3, groups, KS), F32),
            jax.ShapeDtypeStruct((groups, K), F32),
            jax.ShapeDtypeStruct((tiles, 128), F32),
            jax.ShapeDtypeStruct((tiles, 128), F32),
        ),
        in_specs=[pl.BlockSpec(memory_space=pltpu.SMEM)] + [vmem] * 9,
        out_specs=(vmem,) * 8,
        scratch_shapes=[
            pltpu.VMEM((3, RIM, width), BF16),
            pltpu.VMEM((3, RIM, width), BF16),
            pltpu.VMEM((2, RIM, width), BF16),
            pltpu.VMEM((HEAD, width), BF16),
            pltpu.VMEM((HEAD, width), BF16),
            pltpu.VMEM((2, RIM, width), BF16),
            pltpu.VMEM((2, RIM, width), BF16),
            pltpu.VMEM((2 * K, width), BF16),
            pltpu.VMEM((3 * K, width), BF16),
            pltpu.VMEM((RIM, width), BF16),
            pltpu.VMEM((RIM, width), BF16),
            tiled(length + 2 * RIM),
            tiled(length + 2 * RIM),
            tiled(length + 2 * RIM),
            tiled(RIM + HEAD),
            tiled(RIM + HEAD),
            tiled(length),
            tiled(length + RIM),
            tiled(length + RIM),
            tiled(length),
            tiled(length),
            tiled(length + RIM),
            tiled(length + RIM),
            tiled(length + RIM),
            pltpu.VMEM((tiles, per * K, 2 * K), BF16),
            pltpu.VMEM((tiles, per * K, 2 * K), BF16),
            pltpu.VMEM((tiles, per * 8, 2 * K), BF16),
            pltpu.VMEM((6, K, 128), F32),
            pltpu.VMEM((2, 8, 128), F32),
            pltpu.VMEM((KS, length + 2 * RIM, 128), F32),
            pltpu.VMEM((KS, HEAD, 128), F32),
            tiled(24),
            pltpu.VMEM((groups, K), F32),
            pltpu.VMEM((groups, K), F32),
            pltpu.VMEM((groups * 8, K), F32),
            tiled(24),
            pltpu.VMEM((tp_count, 8, 128), F32),
            pltpu.VMEM((INNER, 8, 128), F32),
            pltpu.VMEM((INNER, 8, 128), F32),
            pltpu.VMEM((outer, 8, 128), F32),
            pltpu.VMEM((INNER, 8, 128), F32),
            dma((9,)),
            dma((9,)),
            dma((tp_count,)),
            dma((tp_count,)),
            dma((INNER,)),
            dma((INNER,)),
            dma((outer,)),
            dma((outer,)),
            dma((INNER,)),
            dma((INNER,)),
        ],
        compiler_params=pltpu.CompilerParams(collective_id=0, has_side_effects=True),
        name="operator",
    )(
        lengths,
        q_input,
        k_input,
        v_input,
        resid,
        cotangent,
        short_filter,
        long_filter,
        skip.reshape(1, width),
        gain.reshape(1, width),
    )
    return outs[:6] + (outs[6].reshape(width), outs[7].reshape(width))


def solution(mesh):
    rows = P("ctx", "tp")
    return jax.shard_map(
        shards,
        mesh=mesh,
        in_specs=(
            rows,
            rows,
            rows,
            rows,
            P(),
            P(None, "tp", None),
            P("tp", None),
            P("tp"),
            P("tp"),
            rows,
        ),
        out_specs=(rows, rows, rows, rows, P(None, "tp", None), P("tp", None), P("tp"), P("tp")),
        check_vma=False,
    )
```

```python
import functools

import jax
import jax.numpy as jnp
from jax import lax
from jax.experimental import pallas as pl
from jax.experimental.pallas import tpu as pltpu
from jax.sharding import PartitionSpec as P

C = 4096
GS = 16
K = 128
KS = 7
EPS = 1e-06
INNER = 16
MESH_ID = pl.DeviceIdType.MESH
F32 = jnp.float32
BF16 = jnp.bfloat16
HIGH = lax.Precision.HIGHEST
RIM = 8
HEAD = 16
CHUNKS = 4


def iota(shape, axis):
    return lax.broadcasted_iota(jnp.int32, shape, axis)


def skewed(x):
    return pltpu.roll(x, 0, 1, stride=1, stride_axis=0)


def body(
    count,
    tp_count,
    lengths,
    q_ref,
    k_ref,
    v_ref,
    resid_ref,
    cot_ref,
    short_ref,
    long_ref,
    skip_ref,
    gain_ref,
    normed_out,
    gq_out,
    gk_out,
    gv_out,
    gshort_out,
    glong_out,
    gskip_out,
    ggain_out,
    tail_s,
    tail_r,
    tail2_r,
    headk_r,
    headv_r,
    head_s,
    head_r,
    gext,
    gmx,
    gqs_s,
    gqs_r,
    xq,
    xk,
    xv,
    pk,
    pv,
    sq,
    sk,
    sv,
    mixed_s,
    summed_s,
    eq,
    ek,
    ev,
    fmat,
    umat,
    xmat,
    mats,
    xmasks,
    taps_m,
    prev_m,
    taps_w,
    wfwd,
    wrev,
    glong_s,
    stats,
    xs,
    first,
    second,
    result,
    hs,
    hr,
    ts,
    tr,
    s1,
    r1,
    s2,
    r2,
    s3,
    r3,
    near_s,
    far_s,
    s4,
    r4,
    s5,
    r5,
    normed_b,
    gq_b,
    gk_b,
    gv_b,
    os,
):
    length, width = q_ref.shape
    tiles = width // 128
    per = 128 // GS
    groups = width // GS
    ctx = lax.axis_index("ctx")
    tp = lax.axis_index("tp")
    outer = count // INNER
    hi = ctx // INNER
    lo = ctx % INNER
    total = count * length
    base = ctx * length

    def along(by):
        return (ctx + by + count) % count

    def inner_peer(k):
        return (lo + k) % INNER

    def outer_peer(k):
        return (hi + k) % outer

    def tp_peer(k):
        return (tp + k) % tp_count

    barrier = pltpu.get_barrier_semaphore()
    for by in (1, 2, -1, -2):
        pl.semaphore_signal(barrier, inc=1, device_id={"ctx": along(by)}, device_id_type=MESH_ID)
    for k in range(1, tp_count):
        pl.semaphore_signal(barrier, inc=1, device_id={"tp": tp_peer(k)}, device_id_type=MESH_ID)
    for k in range(1, INNER):
        pl.semaphore_signal(
            barrier, inc=1, device_id={"ctx": hi * INNER + inner_peer(k)}, device_id_type=MESH_ID
        )
    for k in range(1, outer):
        pl.semaphore_signal(
            barrier, inc=1, device_id={"ctx": outer_peer(k) * INNER + lo}, device_id_type=MESH_ID
        )

    def halo(slot, src, dst, by):
        return pltpu.make_async_remote_copy(
            src_ref=src,
            dst_ref=dst,
            send_sem=hs.at[slot],
            recv_sem=hr.at[slot],
            device_id={"ctx": along(by)},
            device_id_type=MESH_ID,
        )

    tails = halo(0, tail_s, tail_r, 1)
    tails2 = halo(1, tail_s.at[pl.ds(1, 2)], tail2_r, 2)
    heads_k = halo(2, k_ref.at[pl.ds(0, HEAD)], headk_r, 1)
    heads_v = halo(3, v_ref.at[pl.ds(0, HEAD)], headv_r, 1)
    heads_back = halo(4, head_s, head_r, -1)
    gm_far = halo(5, gmx.at[:, pl.ds(0, HEAD)], gmx.at[:, pl.ds(2 * K, HEAD)], -2)
    gqs_copy = halo(6, gqs_s, gqs_r, -1)
    each = tiles // CHUNKS
    gated_copies = []
    gm_copies = []
    for c in range(CHUNKS):
        some = pl.ds(c * each, each)
        gated_copies.append(
            halo(
                7 + c,
                gext.at[some, pl.ds(K + HEAD, K - HEAD)],
                gext.at[some, pl.ds(HEAD, K - HEAD)],
                1,
            )
        )
        gm_copies.append(
            halo(7 + CHUNKS + c, gmx.at[some, pl.ds(0, K)], gmx.at[some, pl.ds(K, K)], -1)
        )

    for s, ref in enumerate((q_ref, k_ref, v_ref)):
        tail_s[s] = ref[length - HEAD :, :].astype(F32)[HEAD - RIM :].astype(BF16)
    head_s[0] = k_ref[0:HEAD, :].astype(F32)[:RIM].astype(BF16)
    head_s[1] = v_ref[0:HEAD, :].astype(F32)[:RIM].astype(BF16)

    starts = []
    at = jnp.int32(0)
    for i in range(lengths.shape[0]):
        starts.append(at)
        at = at + lengths[i]

    def position(token):
        begin = jnp.zeros_like(token)
        for start in starts:
            begin = jnp.where(token >= start, start, begin)
        return token - begin

    def flag(cond):
        return jnp.where(cond, 1.0, 0.0).astype(F32)

    token = base - RIM + iota((length + 2 * RIM, 128), 0)
    pos = position(token)
    for j in range(KS):
        taps_m[j] = flag((pos >= j) & (token < total))
    token = base - K + iota((HEAD, 128), 0)
    pos = position(token)
    for j in range(KS):
        prev_m[j] = flag(pos >= j)
    row = iota((K, 128), 0)
    col = iota((K, 128), 1)
    pos = position(base + row)
    mats[0] = flag((col > row) & (pos >= row - col + K))
    mats[1] = flag((col <= row) & (pos >= row - col))

    picks = flag(iota((groups, width), 1) // GS == iota((groups, width), 0)).astype(BF16)
    for s in range(3):
        table = jnp.dot(short_ref[s], picks, preferred_element_type=F32)
        for t in range(tiles):
            taps_w[t, pl.ds(s * 8, KS), :] = table[:, t * 128 : (t + 1) * 128]

    def lanes(t):
        return pl.ds(pl.multiple_of(t * 128, 128), 128)

    def short_sum(buf, t, s, first_row, rows, mask, mask_row):
        result_sum = taps_w[t, pl.ds(s * 8, 1), :] * buf[t, pl.ds(RIM + first_row, rows), :]
        for j in range(1, KS):
            moved = buf[t, pl.ds(RIM + first_row - j, rows), :]
            result_sum = result_sum + taps_w[t, pl.ds(s * 8 + j, 1), :] * (
                moved * mask[j, pl.ds(mask_row, rows), :]
            )
        return result_sum

    rest = length - HEAD

    def gate_main(t, carry):
        xk[t, pl.ds(RIM, length), :] = k_ref[:, lanes(t)].astype(F32)
        xv[t, pl.ds(RIM, length), :] = v_ref[:, lanes(t)].astype(F32)
        ks = short_sum(xk, t, 1, HEAD, rest, taps_m, RIM + HEAD)
        vs = short_sum(xv, t, 2, HEAD, rest, taps_m, RIM + HEAD)
        sk[t, pl.ds(HEAD, rest), :] = ks
        sv[t, pl.ds(HEAD, rest), :] = vs
        gext[t, pl.ds(K + HEAD, rest), :] = (ks * vs).astype(BF16)
        return carry

    lax.fori_loop(0, tiles, gate_main, 0)
    pl.semaphore_wait(barrier, 4 + tp_count - 1 + INNER - 1 + outer - 1)
    tails.start()
    tails2.start()
    heads_k.start()
    heads_v.start()
    heads_back.start()
    for copy in gated_copies:
        copy.start()

    def query_main(t, carry):
        xq[t, pl.ds(RIM, length), :] = q_ref[:, lanes(t)].astype(F32)
        sq[t, pl.ds(HEAD, rest), :] = short_sum(xq, t, 0, HEAD, rest, taps_m, RIM + HEAD)
        return carry

    lax.fori_loop(0, tiles, query_main, 0)

    pos = position(base + col)
    mats[2] = flag((col >= row) & (pos >= col - row))
    token = base + K + col
    pos = position(token)
    mats[3] = flag((col < row) & (pos >= K + col - row) & (token < total))
    near_row = iota((8, 128), 0)
    near_col = iota((8, 128), 1)
    token = base + K + near_col
    pos = position(token)
    xmasks[0] = flag((near_col >= near_row) & (pos >= near_col - near_row) & (token < total))
    token = token + K
    pos = position(token)
    xmasks[1] = flag((near_col < near_row) & (pos >= K + near_col - near_row) & (token < total))

    flip = flag((row + col) % K == 0)
    wfwd[...] = long_ref[...].astype(F32)
    wrev[...] = jnp.dot(long_ref[...], flip.astype(BF16), preferred_element_type=F32)

    def build(t, carry):
        forward = wfwd[pl.ds(pl.multiple_of(t * per, per), per), :]
        backward = wrev[pl.ds(pl.multiple_of(t * per, per), per), :]
        extra = []
        for g in range(per):
            band = skewed(jnp.broadcast_to(backward[g : g + 1, :], (K, K)))
            fmat[t, pl.ds(g * K, K), pl.ds(0, K)] = (band * mats[0]).astype(BF16)
            fmat[t, pl.ds(g * K, K), pl.ds(K, K)] = (band * mats[1]).astype(BF16)
            band = skewed(jnp.broadcast_to(forward[g : g + 1, :], (K, K)))
            umat[t, pl.ds(g * K, K), pl.ds(0, K)] = (band * mats[2]).astype(BF16)
            umat[t, pl.ds(g * K, K), pl.ds(K, K)] = (band * mats[3]).astype(BF16)
            near = band[0:8, :]
            extra.append(jnp.concatenate([near * xmasks[0], near * xmasks[1]], axis=1))
        xmat[t] = jnp.concatenate(extra, axis=0).astype(BF16)
        return carry

    lax.fori_loop(0, tiles, build, 0)
    gmx[:, pl.ds(2 * K + HEAD, K - HEAD), :] = jnp.zeros((tiles, K - HEAD, 128), BF16)

    tails.wait_recv()
    tails2.wait_recv()
    heads_k.wait_recv()
    heads_v.wait_recv()
    heads_back.wait_recv()
    for t in range(tiles):
        part = slice(t * 128, (t + 1) * 128)
        for s, buf in enumerate((xq, xk, xv)):
            buf[t, pl.ds(0, RIM), :] = tail_r[s, :, part].astype(F32)
        for s, (buf, prev, head) in enumerate(((xk, pk, headk_r), (xv, pv, headv_r))):
            buf[t, pl.ds(RIM + length, RIM), :] = head_r[s, :, part].astype(F32)
            prev[t, pl.ds(0, RIM), :] = tail2_r[s, :, part].astype(F32)
            prev[t, pl.ds(RIM, HEAD), :] = head[:, part].astype(F32)

    def gate_rims(t, carry):
        sq[t, pl.ds(0, HEAD), :] = short_sum(xq, t, 0, 0, HEAD, taps_m, RIM)
        ks = short_sum(xk, t, 1, 0, HEAD, taps_m, RIM)
        vs = short_sum(xv, t, 2, 0, HEAD, taps_m, RIM)
        sk[t, pl.ds(0, HEAD), :] = ks
        sv[t, pl.ds(0, HEAD), :] = vs
        gext[t, pl.ds(K, HEAD), :] = (ks * vs).astype(BF16)
        sk[t, pl.ds(length, RIM), :] = short_sum(xk, t, 1, length, RIM, taps_m, RIM + length)
        sv[t, pl.ds(length, RIM), :] = short_sum(xv, t, 2, length, RIM, taps_m, RIM + length)
        ks = short_sum(pk, t, 1, 0, HEAD, prev_m, 0)
        vs = short_sum(pv, t, 2, 0, HEAD, prev_m, 0)
        gext[t, pl.ds(0, HEAD), :] = (ks * vs).astype(BF16)
        return carry

    lax.fori_loop(0, tiles, gate_rims, 0)

    def select(products, rows):
        group = iota((rows, 128), 1) // GS
        picked = products[0:rows]
        for g in range(1, per):
            picked = jnp.where(group == g, products[g * rows : (g + 1) * rows], picked)
        return picked

    def mix(t, carry):
        squares, products = carry
        source = gext[t]
        conv = select(jnp.dot(fmat[t], source, preferred_element_type=F32), K)
        gated = gext[t, pl.ds(K, K), :].astype(F32)
        mixed = conv + skip_ref[:, lanes(t)] * gated
        summed = resid_ref[:, lanes(t)].astype(F32) + sq[t] * mixed
        mixed_s[t] = mixed
        summed_s[t] = summed
        squares = squares + summed * summed
        products = products + gain_ref[:, lanes(t)] * cot_ref[:, lanes(t)].astype(F32) * summed
        return squares, products

    zero = jnp.zeros((length, 128), F32)
    squares, products = zero, zero
    for c in range(CHUNKS):
        gated_copies[c].wait_recv()
        squares, products = lax.fori_loop(c * each, (c + 1) * each, mix, (squares, products))
    squares = jnp.sum(squares.T, axis=0, keepdims=True)
    products = jnp.sum(products.T, axis=0, keepdims=True)
    stats[tp] = jnp.where(near_row == 0, squares, products)

    def share(k):
        return pltpu.make_async_remote_copy(
            src_ref=stats.at[tp],
            dst_ref=stats.at[tp],
            send_sem=ts.at[k],
            recv_sem=tr.at[tp],
            device_id={"tp": tp_peer(k)},
            device_id_type=MESH_ID,
        )

    def arrived(sem, buf, slot):
        pltpu.make_async_copy(buf.at[slot], buf.at[slot], sem.at[slot]).wait()

    for k in range(1, tp_count):
        share(k).start()
    for k in range(1, tp_count):
        arrived(tr, stats, tp_peer(tp_count - k))
    both = stats[0]
    for i in range(1, tp_count):
        both = both + stats[i]
    both = both / (width * tp_count)
    shifted = both[0:1] + EPS
    inverse_row = lax.rsqrt(shifted)
    inverse_row = inverse_row * (1.5 - 0.5 * shifted * inverse_row * inverse_row)
    pull_row = inverse_row * inverse_row * both[1:2]
    inverse = jnp.broadcast_to(inverse_row, (128, length)).T
    pull = jnp.broadcast_to(pull_row, (128, length)).T
    mats[4] = inverse
    mats[5] = pull

    def grads(t, carry):
        inverse = mats[4]
        summed = summed_s[t]
        gain = gain_ref[:, lanes(t)]
        cot = cot_ref[:, lanes(t)].astype(F32)
        normed_b[:, lanes(t)] = (gain * summed * inverse).astype(BF16)
        grad_sum = inverse * (gain * cot - summed * mats[5])
        grad_mixed = (grad_sum * sq[t]).astype(BF16)
        gmx[t, pl.ds(0, K), :] = grad_mixed
        grad_qs = (grad_sum * mixed_s[t]).astype(BF16)
        eq[t, pl.ds(0, length), :] = grad_qs.astype(F32)
        gqs_s[:, lanes(t)] = grad_qs.astype(F32)[:RIM].astype(BF16)
        gated = gext[t, pl.ds(K, K), :].astype(F32)
        xs[8, pl.ds(t, 1), :] = jnp.sum(grad_mixed.astype(F32) * gated, axis=0, keepdims=True)
        xs[9, pl.ds(t, 1), :] = jnp.sum(cot * summed * inverse, axis=0, keepdims=True)
        return carry

    lax.fori_loop(0, tiles, grads, 0)
    gqs_copy.start()
    gm_far.start()
    for copy in gm_copies:
        copy.start()
    stores = [
        pltpu.make_async_copy(buf, out, os.at[i])
        for i, (buf, out) in enumerate(
            ((normed_b, normed_out), (gq_b, gq_out), (gk_b, gk_out), (gv_b, gv_out))
        )
    ]
    stores[0].start()

    def correlate(t, carry):
        grad_mixed = gmx[t, pl.ds(0, K), :]
        source = gext[t]
        group = iota((K, 128), 1) // GS
        left = jnp.concatenate(
            [jnp.where(group == g, grad_mixed, jnp.zeros_like(grad_mixed)) for g in range(per)], axis=0
        )
        cross = lax.dot_general(
            left, source, (((1,), (1,)), ((), ())), preferred_element_type=F32
        )
        for g in range(per):
            block = cross[g * K : (g + 1) * K]
            band = block[:, :K] * mats[0] + block[:, K:] * mats[1]
            folded = band[0:8]
            for a in range(1, K // 8):
                folded = folded + pltpu.roll(band[a * 8 : (a + 1) * 8], K - a * 8, 1)
            glong_s[pl.ds(pl.multiple_of(t * per * 8, 8) + g * 8, 8), :] = folded
        return carry

    lax.fori_loop(0, tiles, correlate, 0)
    folded = glong_s[pl.ds(0, groups, stride=8), :]
    for b in range(1, 8):
        folded = folded + pltpu.roll(glong_s[pl.ds(b, groups, stride=8), :], K - b, 1)
    turned = jnp.dot(folded, flip, precision=HIGH, preferred_element_type=F32)
    for t in range(tiles):
        xs[t] = turned[t * per : (t + 1) * per]
    for i in range(10, INNER):
        xs[i] = jnp.zeros((8, 128), F32)

    def copy_to(src, dst, send, recv, device):
        return pltpu.make_async_remote_copy(
            src_ref=src,
            dst_ref=dst,
            send_sem=send,
            recv_sem=recv,
            device_id={"ctx": device},
            device_id_type=MESH_ID,
        )

    def inner_device(k):
        return hi * INNER + inner_peer(k)

    def outer_device(k):
        return outer_peer(k) * INNER + lo

    def scatter(k):
        return copy_to(xs.at[inner_peer(k)], first.at[lo], s1.at[k], r1.at[lo], inner_device(k))

    def exchange(k):
        return copy_to(second.at[hi], second.at[hi], s2.at[k], r2.at[hi], outer_device(k))

    def gather(k):
        return copy_to(result.at[lo], result.at[lo], s3.at[k], r3.at[lo], inner_device(k))

    def near_sums(k):
        return copy_to(near_s.at[lo], near_s.at[lo], s4.at[k], r4.at[lo], inner_device(k))

    def far_sums(k):
        return copy_to(far_s.at[hi], far_s.at[hi], s5.at[k], r5.at[hi], outer_device(k))

    for k in range(1, INNER):
        scatter(k).start()

    gqs_copy.wait_recv()
    gm_far.wait_recv()

    def rounded(value):
        return value.astype(BF16).astype(F32)

    def back(t, carry):
        upper, lower = carry
        conv = select(
            jnp.dot(umat[t], gmx[t, pl.ds(0, 2 * K), :], preferred_element_type=F32), K
        )
        extra = select(
            jnp.dot(xmat[t], gmx[t, pl.ds(K, 2 * K), :], preferred_element_type=F32), 8
        )
        skip = skip_ref[:, lanes(t)]
        grad_gated = skip * gmx[t, pl.ds(0, K), :].astype(F32) + conv
        ek[t, pl.ds(0, length), :] = rounded(grad_gated * sv[t, pl.ds(0, length), :])
        ev[t, pl.ds(0, length), :] = rounded(grad_gated * sk[t, pl.ds(0, length), :])
        near = gmx[t, pl.ds(K, HEAD), :].astype(F32)[:RIM]
        grad_gated = skip * near + extra
        ek[t, pl.ds(length, RIM), :] = rounded(grad_gated * sv[t, pl.ds(length, RIM), :])
        ev[t, pl.ds(length, RIM), :] = rounded(grad_gated * sk[t, pl.ds(length, RIM), :])
        eq[t, pl.ds(length, RIM), :] = gqs_r[:, lanes(t)].astype(F32)
        blocks = []
        for buf, values in ((eq, xq), (ek, xk), (ev, xv)):
            own = values[t, pl.ds(RIM, length), :]
            for j in range(KS):
                moved = buf[t, pl.ds(j, length), :] * taps_m[j, pl.ds(RIM + j, length), :]
                blocks.append(jnp.sum(moved * own, axis=0, keepdims=True))
            blocks.append(jnp.zeros((1, 128), F32))
        sums = jnp.concatenate(blocks, axis=0)
        high = sums.astype(BF16)
        rest_sums = sums - high.astype(F32)
        middle = rest_sums.astype(BF16)
        low = (rest_sums - middle.astype(F32)).astype(BF16)
        channel = iota((128, 128), 0) // GS + t * per
        spread = flag(channel == iota((128, 128), 1)).astype(BF16)
        spread_high = flag(channel + 64 == iota((128, 128), 1)).astype(BF16)

        def spread_sum(rows, onto):
            parts = jnp.concatenate([high[rows], middle[rows], low[rows]], axis=0)
            parts = jnp.dot(parts, onto, preferred_element_type=F32)
            return parts[0:8] + parts[8:16] + parts[16:24]

        upper = upper + spread_sum(slice(0, 8), spread) + spread_sum(slice(8, 16), spread_high)
        lower = lower + spread_sum(slice(16, 24), spread)
        return upper, lower

    upper = jnp.zeros((8, 128), F32)
    lower = jnp.zeros((8, 128), F32)
    for c in range(CHUNKS):
        gm_copies[c].wait_recv()
        upper, lower = lax.fori_loop(c * each, (c + 1) * each, back, (upper, lower))
        if c == CHUNKS // 2 - 1:
            sums = xs[lo]
            for k in range(1, INNER):
                slot = inner_peer(INNER - k)
                arrived(r1, first, slot)
                sums = sums + first[slot]
            second[hi] = sums
            for k in range(1, outer):
                exchange(k).start()
    near_s[lo, pl.ds(0, 8), :] = upper
    near_s[lo, pl.ds(8, 8), :] = lower
    for k in range(1, INNER):
        near_sums(k).start()
    for k in range(1, outer):
        arrived(r2, second, outer_peer(outer - k))
    sums = second[0]
    for i in range(1, outer):
        sums = sums + second[i]
    result[lo] = sums
    for k in range(1, INNER):
        gather(k).start()

    def streams(t, carry):
        for s, (buf, out) in enumerate(((eq, gq_b), (ek, gk_b), (ev, gv_b))):
            result_sum = jnp.zeros((length, 128), F32)
            for j in range(KS):
                moved = buf[t, pl.ds(j, length), :] * taps_m[j, pl.ds(RIM + j, length), :]
                result_sum = result_sum + taps_w[t, pl.ds(s * 8 + j, 1), :] * moved
            out[:, lanes(t)] = result_sum.astype(BF16)
        return carry

    lax.fori_loop(0, tiles, streams, 0)
    for store in stores[1:]:
        store.start()

    for k in range(1, INNER):
        arrived(r4, near_s, inner_peer(INNER - k))
    sums = near_s[0]
    for i in range(1, INNER):
        sums = sums + near_s[i]
    far_s[hi] = sums
    for k in range(1, outer):
        far_sums(k).start()

    for k in range(1, INNER):
        arrived(r3, result, inner_peer(INNER - k))
    for t in range(tiles):
        glong_out[pl.ds(t * per, per), :] = result[t]
    gskip_out[...] = result[8]
    ggain_out[...] = result[9]
    for copy in [tails, tails2, heads_k, heads_v, heads_back, gm_far, gqs_copy] + gated_copies + gm_copies:
        copy.wait_send()
    for k in range(1, tp_count):
        share(k).wait_send()
    for k in range(1, INNER):
        scatter(k).wait_send()
        gather(k).wait_send()
        near_sums(k).wait_send()
    for k in range(1, outer):
        exchange(k).wait_send()

    for k in range(1, outer):
        arrived(r5, far_s, outer_peer(outer - k))
    sums = far_s[0]
    for i in range(1, outer):
        sums = sums + far_s[i]
    gshort_out[0] = sums[:KS, :groups]
    gshort_out[1] = sums[:KS, 64 : 64 + groups]
    gshort_out[2] = sums[8 : 8 + KS, :groups]
    for k in range(1, outer):
        far_sums(k).wait_send()
    for store in stores:
        store.wait()


def finish(*refs):
    half = (len(refs) - 2) // 3
    came, left = refs[-2:]
    bufs = refs[2 * half : 3 * half]
    reads = [pltpu.make_async_copy(refs[i], bufs[i], came.at[i]) for i in range(half)]
    writes = [pltpu.make_async_copy(bufs[i], refs[half + i], left.at[i]) for i in range(half)]
    for copy in reads:
        copy.start()
    for read, write in zip(reads, writes):
        read.wait()
        write.start()
    for copy in writes:
        copy.wait()


def shards(
    q_input, k_input, v_input, resid, lengths, short_filter, long_filter, skip, gain, cotangent
):
    length, width = q_input.shape
    tiles = width // 128
    groups = width // GS
    per = 128 // GS
    count = lax.axis_size("ctx")
    tp_count = lax.axis_size("tp")
    outer = count // INNER
    vmem = pl.BlockSpec(memory_space=pltpu.VMEM)
    large = jax.ShapeDtypeStruct((length, width), BF16)

    def tiled(rows):
        return pltpu.VMEM((tiles, rows, 128), F32)

    dma = pltpu.SemaphoreType.DMA
    outs = pl.pallas_call(
        functools.partial(body, count, tp_count),
        out_shape=(
            large,
            large,
            large,
            large,
            jax.ShapeDtypeStruct((3, KS, groups), F32),
            jax.ShapeDtypeStruct((groups, K), F32),
            jax.ShapeDtypeStruct((tiles, 128), F32),
            jax.ShapeDtypeStruct((tiles, 128), F32),
        ),
        in_specs=[pl.BlockSpec(memory_space=pltpu.SMEM)] + [vmem] * 9,
        out_specs=(pl.BlockSpec(memory_space=pl.ANY),) * 4 + (vmem,) * 4,
        scratch_shapes=[
            pltpu.VMEM((3, RIM, width), BF16),
            pltpu.VMEM((3, RIM, width), BF16),
            pltpu.VMEM((2, RIM, width), BF16),
            pltpu.VMEM((HEAD, width), BF16),
            pltpu.VMEM((HEAD, width), BF16),
            pltpu.VMEM((2, RIM, width), BF16),
            pltpu.VMEM((2, RIM, width), BF16),
            pltpu.VMEM((tiles, 2 * K, 128), BF16),
            pltpu.VMEM((tiles, 3 * K, 128), BF16),
            pltpu.VMEM((RIM, width), BF16),
            pltpu.VMEM((RIM, width), BF16),
            tiled(length + 2 * RIM),
            tiled(length + 2 * RIM),
            tiled(length + 2 * RIM),
            tiled(RIM + HEAD),
            tiled(RIM + HEAD),
            tiled(length),
            tiled(length + RIM),
            tiled(length + RIM),
            tiled(length),
            tiled(length),
            tiled(length + RIM),
            tiled(length + RIM),
            tiled(length + RIM),
            pltpu.VMEM((tiles, per * K, 2 * K), BF16),
            pltpu.VMEM((tiles, per * K, 2 * K), BF16),
            pltpu.VMEM((tiles, per * 8, 2 * K), BF16),
            pltpu.VMEM((6, K, 128), F32),
            pltpu.VMEM((2, 8, 128), F32),
            pltpu.VMEM((KS, length + 2 * RIM, 128), F32),
            pltpu.VMEM((KS, HEAD, 128), F32),
            tiled(24),
            pltpu.VMEM((groups, K), F32),
            pltpu.VMEM((groups, K), F32),
            pltpu.VMEM((groups * 8, K), F32),
            pltpu.VMEM((tp_count, 8, 128), F32),
            pltpu.VMEM((INNER, 8, 128), F32),
            pltpu.VMEM((INNER, 8, 128), F32),
            pltpu.VMEM((outer, 8, 128), F32),
            pltpu.VMEM((INNER, 8, 128), F32),
            dma((7 + 2 * CHUNKS,)),
            dma((7 + 2 * CHUNKS,)),
            dma((tp_count,)),
            dma((tp_count,)),
            dma((INNER,)),
            dma((INNER,)),
            dma((outer,)),
            dma((outer,)),
            dma((INNER,)),
            dma((INNER,)),
            pltpu.VMEM((INNER, 16, 128), F32),
            pltpu.VMEM((outer, 16, 128), F32),
            dma((INNER,)),
            dma((INNER,)),
            dma((outer,)),
            dma((outer,)),
            pltpu.VMEM((length, width), BF16),
            pltpu.VMEM((length, width), BF16),
            pltpu.VMEM((length, width), BF16),
            pltpu.VMEM((length, width), BF16),
            dma((4,)),
        ],
        compiler_params=pltpu.CompilerParams(collective_id=0, has_side_effects=True),
        name="operator",
    )(
        lengths,
        q_input,
        k_input,
        v_input,
        resid,
        cotangent,
        jnp.transpose(short_filter, (0, 2, 1)),
        long_filter,
        skip.reshape(1, width),
        gain.reshape(1, width),
    )
    outs = pl.pallas_call(
        finish,
        out_shape=tuple(jax.ShapeDtypeStruct(out.shape, out.dtype) for out in outs),
        in_specs=[pl.BlockSpec(memory_space=pl.ANY)] * 8,
        out_specs=(pl.BlockSpec(memory_space=pl.ANY),) * 8,
        scratch_shapes=[pltpu.VMEM(out.shape, out.dtype) for out in outs] + [dma((8,)), dma((8,))],
        name="finish",
    )(*outs)
    return outs[:4] + (
        jnp.transpose(outs[4], (0, 2, 1)),
        outs[5],
        outs[6].reshape(width),
        outs[7].reshape(width),
    )


def solution(mesh):
    rows = P("ctx", "tp")
    return jax.shard_map(
        shards,
        mesh=mesh,
        in_specs=(
            rows,
            rows,
            rows,
            rows,
            P(),
            P(None, "tp", None),
            P("tp", None),
            P("tp"),
            P("tp"),
            rows,
        ),
        out_specs=(rows, rows, rows, rows, P(None, "tp", None), P("tp", None), P("tp"), P("tp")),
        check_vma=False,
    )
```

```python
import functools

import jax
import jax.numpy as jnp
from jax import lax
from jax.experimental import pallas as pl
from jax.experimental.pallas import tpu as pltpu
from jax.sharding import PartitionSpec as P

C = 4096
GS = 16
K = 128
KS = 7
EPS = 1e-06
INNER = 16
MESH_ID = pl.DeviceIdType.MESH
F32 = jnp.float32
BF16 = jnp.bfloat16
HIGH = lax.Precision.HIGHEST
RIM = 8
HEAD = 16
CHUNKS = 4


def iota(shape, axis):
    return lax.broadcasted_iota(jnp.int32, shape, axis)


def skewed(x):
    return pltpu.roll(x, 0, 1, stride=1, stride_axis=0)


def body(
    count,
    tp_count,
    lengths,
    q_ref,
    k_ref,
    v_ref,
    resid_ref,
    cot_ref,
    short_ref,
    long_ref,
    skip_ref,
    gain_ref,
    normed_out,
    gq_out,
    gk_out,
    gv_out,
    gshort_out,
    glong_out,
    gskip_out,
    ggain_out,
    tail_s,
    tail_r,
    tail2_r,
    headk_r,
    headv_r,
    head_s,
    head_r,
    gext,
    gmx,
    gqs_s,
    gqs_r,
    xq,
    xk,
    xv,
    pk,
    pv,
    sq,
    sk,
    sv,
    mixed_s,
    summed_s,
    eq,
    ek,
    ev,
    fmat,
    umat,
    xmat,
    mats,
    xmasks,
    taps_m,
    prev_m,
    taps_w,
    wfwd,
    wrev,
    glong_s,
    stats,
    xs,
    first,
    second,
    result,
    hs,
    hr,
    ts,
    tr,
    s1,
    r1,
    s2,
    r2,
    s3,
    r3,
    near_s,
    far_s,
    tsum,
    s4,
    r4,
    s5,
    r5,
    normed_b,
    gq_b,
    gk_b,
    gv_b,
    os,
):
    length, width = q_ref.shape
    tiles = width // 128
    per = 128 // GS
    groups = width // GS
    ctx = lax.axis_index("ctx")
    tp = lax.axis_index("tp")
    outer = count // INNER
    hi = ctx // INNER
    lo = ctx % INNER
    total = count * length
    base = ctx * length

    def along(by):
        return (ctx + by + count) % count

    def inner_peer(k):
        return (lo + k) % INNER

    def outer_peer(k):
        return (hi + k) % outer

    def tp_peer(k):
        return (tp + k) % tp_count

    barrier = pltpu.get_barrier_semaphore()
    for by in (1, 2, -1, -2):
        pl.semaphore_signal(barrier, inc=1, device_id={"ctx": along(by)}, device_id_type=MESH_ID)
    for k in range(1, tp_count):
        pl.semaphore_signal(barrier, inc=1, device_id={"tp": tp_peer(k)}, device_id_type=MESH_ID)
    for k in range(1, INNER):
        pl.semaphore_signal(
            barrier, inc=1, device_id={"ctx": hi * INNER + inner_peer(k)}, device_id_type=MESH_ID
        )
    for k in range(1, outer):
        pl.semaphore_signal(
            barrier, inc=1, device_id={"ctx": outer_peer(k) * INNER + lo}, device_id_type=MESH_ID
        )

    def halo(slot, src, dst, by):
        return pltpu.make_async_remote_copy(
            src_ref=src,
            dst_ref=dst,
            send_sem=hs.at[slot],
            recv_sem=hr.at[slot],
            device_id={"ctx": along(by)},
            device_id_type=MESH_ID,
        )

    tails = halo(0, tail_s, tail_r, 1)
    tails2 = halo(1, tail_s.at[pl.ds(1, 2)], tail2_r, 2)
    heads_k = halo(2, k_ref.at[pl.ds(0, HEAD)], headk_r, 1)
    heads_v = halo(3, v_ref.at[pl.ds(0, HEAD)], headv_r, 1)
    heads_back = halo(4, head_s, head_r, -1)
    gm_far = halo(5, gmx.at[:, pl.ds(0, HEAD)], gmx.at[:, pl.ds(2 * K, HEAD)], -2)
    gqs_copy = halo(6, gqs_s, gqs_r, -1)
    each = tiles // CHUNKS
    gated_copies = []
    gm_copies = []
    for c in range(CHUNKS):
        some = pl.ds(c * each, each)
        gated_copies.append(
            halo(
                7 + c,
                gext.at[some, pl.ds(K + HEAD, K - HEAD)],
                gext.at[some, pl.ds(HEAD, K - HEAD)],
                1,
            )
        )
        gm_copies.append(
            halo(7 + CHUNKS + c, gmx.at[some, pl.ds(0, K)], gmx.at[some, pl.ds(K, K)], -1)
        )

    for s, ref in enumerate((q_ref, k_ref, v_ref)):
        tail_s[s] = ref[length - HEAD :, :].astype(F32)[HEAD - RIM :].astype(BF16)
    head_s[0] = k_ref[0:HEAD, :].astype(F32)[:RIM].astype(BF16)
    head_s[1] = v_ref[0:HEAD, :].astype(F32)[:RIM].astype(BF16)

    starts = []
    at = jnp.int32(0)
    for i in range(lengths.shape[0]):
        starts.append(at)
        at = at + lengths[i]

    def position(token):
        begin = jnp.zeros_like(token)
        for start in starts:
            begin = jnp.where(token >= start, start, begin)
        return token - begin

    def flag(cond):
        return jnp.where(cond, 1.0, 0.0).astype(F32)

    token = base - RIM + iota((length + 2 * RIM, 128), 0)
    pos = position(token)
    for j in range(KS):
        taps_m[j] = flag((pos >= j) & (token < total))
    token = base - K + iota((HEAD, 128), 0)
    pos = position(token)
    for j in range(KS):
        prev_m[j] = flag(pos >= j)
    row = iota((K, 128), 0)
    col = iota((K, 128), 1)
    pos = position(base + row)
    mats[0] = flag((col > row) & (pos >= row - col + K))
    mats[1] = flag((col <= row) & (pos >= row - col))

    picks = flag(iota((groups, width), 1) // GS == iota((groups, width), 0)).astype(BF16)
    for s in range(3):
        table = jnp.dot(short_ref[s], picks, preferred_element_type=F32)
        for t in range(tiles):
            taps_w[t, pl.ds(s * 8, KS), :] = table[:, t * 128 : (t + 1) * 128]

    def lanes(t):
        return pl.ds(pl.multiple_of(t * 128, 128), 128)

    def short_sum(buf, t, s, first_row, rows, mask, mask_row):
        result_sum = taps_w[t, pl.ds(s * 8, 1), :] * buf[t, pl.ds(RIM + first_row, rows), :]
        for j in range(1, KS):
            moved = buf[t, pl.ds(RIM + first_row - j, rows), :]
            result_sum = result_sum + taps_w[t, pl.ds(s * 8 + j, 1), :] * (
                moved * mask[j, pl.ds(mask_row, rows), :]
            )
        return result_sum

    rest = length - HEAD

    def gate_main(t, carry):
        xk[t, pl.ds(RIM, length), :] = k_ref[:, lanes(t)].astype(F32)
        xv[t, pl.ds(RIM, length), :] = v_ref[:, lanes(t)].astype(F32)
        ks = short_sum(xk, t, 1, HEAD, rest, taps_m, RIM + HEAD)
        vs = short_sum(xv, t, 2, HEAD, rest, taps_m, RIM + HEAD)
        sk[t, pl.ds(HEAD, rest), :] = ks
        sv[t, pl.ds(HEAD, rest), :] = vs
        gext[t, pl.ds(K + HEAD, rest), :] = (ks * vs).astype(BF16)
        return carry

    lax.fori_loop(0, tiles, gate_main, 0)
    pl.semaphore_wait(barrier, 4 + tp_count - 1 + INNER - 1 + outer - 1)
    tails.start()
    tails2.start()
    heads_k.start()
    heads_v.start()
    for copy in gated_copies:
        copy.start()
    heads_back.start()

    def query_main(t, carry):
        xq[t, pl.ds(RIM, length), :] = q_ref[:, lanes(t)].astype(F32)
        sq[t, pl.ds(HEAD, rest), :] = short_sum(xq, t, 0, HEAD, rest, taps_m, RIM + HEAD)
        return carry

    lax.fori_loop(0, tiles, query_main, 0)

    pos = position(base + col)
    mats[2] = flag((col >= row) & (pos >= col - row))
    token = base + K + col
    pos = position(token)
    mats[3] = flag((col < row) & (pos >= K + col - row) & (token < total))
    near_row = iota((8, 128), 0)
    near_col = iota((8, 128), 1)
    token = base + K + near_col
    pos = position(token)
    xmasks[0] = flag((near_col >= near_row) & (pos >= near_col - near_row) & (token < total))
    token = token + K
    pos = position(token)
    xmasks[1] = flag((near_col < near_row) & (pos >= K + near_col - near_row) & (token < total))

    flip = flag((row + col) % K == 0)
    wfwd[...] = long_ref[...].astype(F32)
    wrev[...] = jnp.dot(long_ref[...], flip.astype(BF16), preferred_element_type=F32)

    def build(t, carry):
        forward = wfwd[pl.ds(pl.multiple_of(t * per, per), per), :]
        backward = wrev[pl.ds(pl.multiple_of(t * per, per), per), :]
        extra = []
        for g in range(per):
            band = skewed(jnp.broadcast_to(backward[g : g + 1, :], (K, K)))
            fmat[t, pl.ds(g * K, K), pl.ds(0, K)] = (band * mats[0]).astype(BF16)
            fmat[t, pl.ds(g * K, K), pl.ds(K, K)] = (band * mats[1]).astype(BF16)
            band = skewed(jnp.broadcast_to(forward[g : g + 1, :], (K, K)))
            umat[t, pl.ds(g * K, K), pl.ds(0, K)] = (band * mats[2]).astype(BF16)
            umat[t, pl.ds(g * K, K), pl.ds(K, K)] = (band * mats[3]).astype(BF16)
            near = band[0:8, :]
            extra.append(jnp.concatenate([near * xmasks[0], near * xmasks[1]], axis=1))
        xmat[t] = jnp.concatenate(extra, axis=0).astype(BF16)
        return carry

    lax.fori_loop(0, tiles, build, 0)
    gmx[:, pl.ds(2 * K + HEAD, K - HEAD), :] = jnp.zeros((tiles, K - HEAD, 128), BF16)

    tails.wait_recv()
    tails2.wait_recv()
    heads_k.wait_recv()
    heads_v.wait_recv()
    for t in range(tiles):
        part = slice(t * 128, (t + 1) * 128)
        for s, buf in enumerate((xq, xk, xv)):
            buf[t, pl.ds(0, RIM), :] = tail_r[s, :, part].astype(F32)
        for s, (buf, prev, head) in enumerate(((xk, pk, headk_r), (xv, pv, headv_r))):
            prev[t, pl.ds(0, RIM), :] = tail2_r[s, :, part].astype(F32)
            prev[t, pl.ds(RIM, HEAD), :] = head[:, part].astype(F32)

    def gate_rims(t, carry):
        sq[t, pl.ds(0, HEAD), :] = short_sum(xq, t, 0, 0, HEAD, taps_m, RIM)
        ks = short_sum(xk, t, 1, 0, HEAD, taps_m, RIM)
        vs = short_sum(xv, t, 2, 0, HEAD, taps_m, RIM)
        sk[t, pl.ds(0, HEAD), :] = ks
        sv[t, pl.ds(0, HEAD), :] = vs
        gext[t, pl.ds(K, HEAD), :] = (ks * vs).astype(BF16)
        ks = short_sum(pk, t, 1, 0, HEAD, prev_m, 0)
        vs = short_sum(pv, t, 2, 0, HEAD, prev_m, 0)
        gext[t, pl.ds(0, HEAD), :] = (ks * vs).astype(BF16)
        return carry

    lax.fori_loop(0, tiles, gate_rims, 0)

    def select(products, rows):
        group = iota((rows, 128), 1) // GS
        picked = products[0:rows]
        for g in range(1, per):
            picked = jnp.where(group == g, products[g * rows : (g + 1) * rows], picked)
        return picked

    def mix(t, carry):
        squares, products = carry
        source = gext[t]
        conv = select(jnp.dot(fmat[t], source, preferred_element_type=F32), K)
        gated = gext[t, pl.ds(K, K), :].astype(F32)
        mixed = conv + skip_ref[:, lanes(t)] * gated
        summed = resid_ref[:, lanes(t)].astype(F32) + sq[t] * mixed
        mixed_s[t] = mixed
        summed_s[t] = summed
        squares = squares + summed * summed
        products = products + gain_ref[:, lanes(t)] * cot_ref[:, lanes(t)].astype(F32) * summed
        return squares, products

    zero = jnp.zeros((length, 128), F32)
    squares, products = zero, zero
    for c in range(CHUNKS):
        gated_copies[c].wait_recv()
        squares, products = lax.fori_loop(c * each, (c + 1) * each, mix, (squares, products))
    squares = jnp.sum(squares.T, axis=0, keepdims=True)
    products = jnp.sum(products.T, axis=0, keepdims=True)
    stats[tp] = jnp.where(near_row == 0, squares, products)

    def share(k):
        return pltpu.make_async_remote_copy(
            src_ref=stats.at[tp],
            dst_ref=stats.at[tp],
            send_sem=ts.at[k],
            recv_sem=tr.at[tp],
            device_id={"tp": tp_peer(k)},
            device_id_type=MESH_ID,
        )

    def arrived(sem, buf, slot):
        pltpu.make_async_copy(buf.at[slot], buf.at[slot], sem.at[slot]).wait()

    for k in range(1, tp_count):
        share(k).start()
    for k in range(1, tp_count):
        arrived(tr, stats, tp_peer(tp_count - k))
    both = stats[0]
    for i in range(1, tp_count):
        both = both + stats[i]
    both = both / (width * tp_count)
    shifted = both[0:1] + EPS
    inverse_row = lax.rsqrt(shifted)
    inverse_row = inverse_row * (1.5 - 0.5 * shifted * inverse_row * inverse_row)
    pull_row = inverse_row * inverse_row * both[1:2]
    inverse = jnp.broadcast_to(inverse_row, (128, length)).T
    pull = jnp.broadcast_to(pull_row, (128, length)).T
    mats[4] = inverse
    mats[5] = pull

    def grads(t, carry):
        inverse = mats[4]
        summed = summed_s[t]
        gain = gain_ref[:, lanes(t)]
        cot = cot_ref[:, lanes(t)].astype(F32)
        normed_b[:, lanes(t)] = (gain * summed * inverse).astype(BF16)
        grad_sum = inverse * (gain * cot - summed * mats[5])
        grad_mixed = (grad_sum * sq[t]).astype(BF16)
        gmx[t, pl.ds(0, K), :] = grad_mixed
        grad_qs = (grad_sum * mixed_s[t]).astype(BF16)
        eq[t, pl.ds(0, length), :] = grad_qs.astype(F32)
        gqs_s[:, lanes(t)] = grad_qs.astype(F32)[:RIM].astype(BF16)
        gated = gext[t, pl.ds(K, K), :].astype(F32)
        xs[8, pl.ds(t, 1), :] = jnp.sum(grad_mixed.astype(F32) * gated, axis=0, keepdims=True)
        xs[9, pl.ds(t, 1), :] = jnp.sum(cot * summed * inverse, axis=0, keepdims=True)
        return carry

    lax.fori_loop(0, tiles, grads, 0)
    gqs_copy.start()
    gm_far.start()
    for copy in gm_copies:
        copy.start()
    stores = [
        pltpu.make_async_copy(buf, out, os.at[i])
        for i, (buf, out) in enumerate(
            ((normed_b, normed_out), (gq_b, gq_out), (gk_b, gk_out), (gv_b, gv_out))
        )
    ]
    stores[0].start()

    def correlate(t, carry):
        grad_mixed = gmx[t, pl.ds(0, K), :]
        source = gext[t]
        group = iota((K, 128), 1) // GS
        left = jnp.concatenate(
            [jnp.where(group == g, grad_mixed, jnp.zeros_like(grad_mixed)) for g in range(per)], axis=0
        )
        cross = lax.dot_general(
            left, source, (((1,), (1,)), ((), ())), preferred_element_type=F32
        )
        for g in range(per):
            block = cross[g * K : (g + 1) * K]
            band = block[:, :K] * mats[0] + block[:, K:] * mats[1]
            folded = band[0:8]
            for a in range(1, K // 8):
                folded = folded + pltpu.roll(band[a * 8 : (a + 1) * 8], K - a * 8, 1)
            glong_s[pl.ds(pl.multiple_of(t * per * 8, 8) + g * 8, 8), :] = folded
        return carry

    lax.fori_loop(0, tiles, correlate, 0)
    folded = glong_s[pl.ds(0, groups, stride=8), :]
    for b in range(1, 8):
        folded = folded + pltpu.roll(glong_s[pl.ds(b, groups, stride=8), :], K - b, 1)
    turned = jnp.dot(folded, flip, precision=HIGH, preferred_element_type=F32)
    for t in range(tiles):
        xs[t] = turned[t * per : (t + 1) * per]
    for i in range(10, INNER):
        xs[i] = jnp.zeros((8, 128), F32)
    tsum[...] = jnp.zeros_like(tsum)

    def copy_to(src, dst, send, recv, device):
        return pltpu.make_async_remote_copy(
            src_ref=src,
            dst_ref=dst,
            send_sem=send,
            recv_sem=recv,
            device_id={"ctx": device},
            device_id_type=MESH_ID,
        )

    def inner_device(k):
        return hi * INNER + inner_peer(k)

    def outer_device(k):
        return outer_peer(k) * INNER + lo

    def scatter(k):
        return copy_to(xs.at[inner_peer(k)], first.at[lo], s1.at[k], r1.at[lo], inner_device(k))

    def exchange(k):
        return copy_to(second.at[hi], second.at[hi], s2.at[k], r2.at[hi], outer_device(k))

    def gather(k):
        return copy_to(result.at[lo], result.at[lo], s3.at[k], r3.at[lo], inner_device(k))

    def near_sums(k):
        return copy_to(near_s.at[lo], near_s.at[lo], s4.at[k], r4.at[lo], inner_device(k))

    def far_sums(k):
        return copy_to(far_s.at[hi], far_s.at[hi], s5.at[k], r5.at[hi], outer_device(k))

    for k in range(1, INNER):
        scatter(k).start()

    heads_back.wait_recv()

    def gate_next(t, carry):
        for s, buf in enumerate((xk, xv)):
            buf[t, pl.ds(RIM + length, RIM), :] = head_r[s, :, lanes(t)].astype(F32)
        sk[t, pl.ds(length, RIM), :] = short_sum(xk, t, 1, length, RIM, taps_m, RIM + length)
        sv[t, pl.ds(length, RIM), :] = short_sum(xv, t, 2, length, RIM, taps_m, RIM + length)
        return carry

    lax.fori_loop(0, tiles, gate_next, 0)
    gqs_copy.wait_recv()
    gm_far.wait_recv()

    def rounded(value):
        return value.astype(BF16).astype(F32)

    def back(t, carry):
        conv = select(
            jnp.dot(umat[t], gmx[t, pl.ds(0, 2 * K), :], preferred_element_type=F32), K
        )
        extra = select(
            jnp.dot(xmat[t], gmx[t, pl.ds(K, 2 * K), :], preferred_element_type=F32), 8
        )
        skip = skip_ref[:, lanes(t)]
        grad_gated = skip * gmx[t, pl.ds(0, K), :].astype(F32) + conv
        ek[t, pl.ds(0, length), :] = rounded(grad_gated * sv[t, pl.ds(0, length), :])
        ev[t, pl.ds(0, length), :] = rounded(grad_gated * sk[t, pl.ds(0, length), :])
        near = gmx[t, pl.ds(K, HEAD), :].astype(F32)[:RIM]
        grad_gated = skip * near + extra
        ek[t, pl.ds(length, RIM), :] = rounded(grad_gated * sv[t, pl.ds(length, RIM), :])
        ev[t, pl.ds(length, RIM), :] = rounded(grad_gated * sk[t, pl.ds(length, RIM), :])
        eq[t, pl.ds(length, RIM), :] = gqs_r[:, lanes(t)].astype(F32)
        for s, (buf, values) in enumerate(((eq, xq), (ek, xk), (ev, xv))):
            own = values[t, pl.ds(RIM, length), :]
            for j in range(KS):
                moved = buf[t, pl.ds(j, length), :] * taps_m[j, pl.ds(RIM + j, length), :]
                tsum[t, pl.ds(s * 8 + j, 1), :] = jnp.sum(moved * own, axis=0, keepdims=True)
        return carry

    for c in range(CHUNKS):
        gm_copies[c].wait_recv()
        lax.fori_loop(c * each, (c + 1) * each, back, 0)
    spread_sums = jnp.zeros((72, 128), F32)
    for t in range(tiles):
        sums = tsum[t]
        high = sums.astype(BF16).astype(F32)
        middle = (sums - high).astype(BF16).astype(F32)
        parts = jnp.concatenate([high, middle, sums - high - middle], axis=0).astype(BF16)
        spread = flag(row // GS + t * per == col).astype(BF16)
        spread_sums = spread_sums + jnp.dot(parts, spread, preferred_element_type=F32)
    spread_sums = spread_sums[0:24] + spread_sums[24:48] + spread_sums[48:72]
    near_s[lo, pl.ds(0, 8), :] = spread_sums[0:8] + pltpu.roll(spread_sums[8:16], 64, 1)
    near_s[lo, pl.ds(8, 8), :] = spread_sums[16:24]
    for k in range(1, INNER):
        near_sums(k).start()
    sums = xs[lo]
    for k in range(1, INNER):
        slot = inner_peer(INNER - k)
        arrived(r1, first, slot)
        sums = sums + first[slot]
    second[hi] = sums
    for k in range(1, outer):
        exchange(k).start()

    def streams(t, carry):
        for s, (buf, out) in enumerate(((eq, gq_b), (ek, gk_b), (ev, gv_b))):
            result_sum = jnp.zeros((length, 128), F32)
            for j in range(KS):
                moved = buf[t, pl.ds(j, length), :] * taps_m[j, pl.ds(RIM + j, length), :]
                result_sum = result_sum + taps_w[t, pl.ds(s * 8 + j, 1), :] * moved
            out[:, lanes(t)] = result_sum.astype(BF16)
        return carry

    lax.fori_loop(0, tiles, streams, 0)
    for store in stores[1:]:
        store.start()

    for k in range(1, outer):
        arrived(r2, second, outer_peer(outer - k))
    sums = second[0]
    for i in range(1, outer):
        sums = sums + second[i]
    result[lo] = sums
    for k in range(1, INNER):
        gather(k).start()

    for k in range(1, INNER):
        arrived(r4, near_s, inner_peer(INNER - k))
    sums = near_s[0]
    for i in range(1, INNER):
        sums = sums + near_s[i]
    far_s[hi] = sums
    for k in range(1, outer):
        far_sums(k).start()

    for k in range(1, INNER):
        arrived(r3, result, inner_peer(INNER - k))
    for t in range(tiles):
        glong_out[pl.ds(t * per, per), :] = result[t]
    gskip_out[...] = result[8]
    ggain_out[...] = result[9]
    for copy in [tails, tails2, heads_k, heads_v, heads_back, gm_far, gqs_copy] + gated_copies + gm_copies:
        copy.wait_send()
    for k in range(1, tp_count):
        share(k).wait_send()
    for k in range(1, INNER):
        scatter(k).wait_send()
        gather(k).wait_send()
        near_sums(k).wait_send()
    for k in range(1, outer):
        exchange(k).wait_send()

    for k in range(1, outer):
        arrived(r5, far_s, outer_peer(outer - k))
    sums = far_s[0]
    for i in range(1, outer):
        sums = sums + far_s[i]
    gshort_out[0] = sums[:KS, :groups]
    gshort_out[1] = sums[:KS, 64 : 64 + groups]
    gshort_out[2] = sums[8 : 8 + KS, :groups]
    for k in range(1, outer):
        far_sums(k).wait_send()
    for store in stores:
        store.wait()


def finish(*refs):
    half = (len(refs) - 2) // 3
    came, left = refs[-2:]
    bufs = refs[2 * half : 3 * half]
    reads = [pltpu.make_async_copy(refs[i], bufs[i], came.at[i]) for i in range(half)]
    writes = [pltpu.make_async_copy(bufs[i], refs[half + i], left.at[i]) for i in range(half)]
    for copy in reads:
        copy.start()
    for read, write in zip(reads, writes):
        read.wait()
        write.start()
    for copy in writes:
        copy.wait()


def shards(
    q_input, k_input, v_input, resid, lengths, short_filter, long_filter, skip, gain, cotangent
):
    length, width = q_input.shape
    tiles = width // 128
    groups = width // GS
    per = 128 // GS
    count = lax.axis_size("ctx")
    tp_count = lax.axis_size("tp")
    outer = count // INNER
    vmem = pl.BlockSpec(memory_space=pltpu.VMEM)
    large = jax.ShapeDtypeStruct((length, width), BF16)

    def tiled(rows):
        return pltpu.VMEM((tiles, rows, 128), F32)

    dma = pltpu.SemaphoreType.DMA
    outs = pl.pallas_call(
        functools.partial(body, count, tp_count),
        out_shape=(
            large,
            large,
            large,
            large,
            jax.ShapeDtypeStruct((3, KS, groups), F32),
            jax.ShapeDtypeStruct((groups, K), F32),
            jax.ShapeDtypeStruct((tiles, 128), F32),
            jax.ShapeDtypeStruct((tiles, 128), F32),
        ),
        in_specs=[pl.BlockSpec(memory_space=pltpu.SMEM)] + [vmem] * 9,
        out_specs=(pl.BlockSpec(memory_space=pl.ANY),) * 4 + (vmem,) * 4,
        scratch_shapes=[
            pltpu.VMEM((3, RIM, width), BF16),
            pltpu.VMEM((3, RIM, width), BF16),
            pltpu.VMEM((2, RIM, width), BF16),
            pltpu.VMEM((HEAD, width), BF16),
            pltpu.VMEM((HEAD, width), BF16),
            pltpu.VMEM((2, RIM, width), BF16),
            pltpu.VMEM((2, RIM, width), BF16),
            pltpu.VMEM((tiles, 2 * K, 128), BF16),
            pltpu.VMEM((tiles, 3 * K, 128), BF16),
            pltpu.VMEM((RIM, width), BF16),
            pltpu.VMEM((RIM, width), BF16),
            tiled(length + 2 * RIM),
            tiled(length + 2 * RIM),
            tiled(length + 2 * RIM),
            tiled(RIM + HEAD),
            tiled(RIM + HEAD),
            tiled(length),
            tiled(length + RIM),
            tiled(length + RIM),
            tiled(length),
            tiled(length),
            tiled(length + RIM),
            tiled(length + RIM),
            tiled(length + RIM),
            pltpu.VMEM((tiles, per * K, 2 * K), BF16),
            pltpu.VMEM((tiles, per * K, 2 * K), BF16),
            pltpu.VMEM((tiles, per * 8, 2 * K), BF16),
            pltpu.VMEM((6, K, 128), F32),
            pltpu.VMEM((2, 8, 128), F32),
            pltpu.VMEM((KS, length + 2 * RIM, 128), F32),
            pltpu.VMEM((KS, HEAD, 128), F32),
            tiled(24),
            pltpu.VMEM((groups, K), F32),
            pltpu.VMEM((groups, K), F32),
            pltpu.VMEM((groups * 8, K), F32),
            pltpu.VMEM((tp_count, 8, 128), F32),
            pltpu.VMEM((INNER, 8, 128), F32),
            pltpu.VMEM((INNER, 8, 128), F32),
            pltpu.VMEM((outer, 8, 128), F32),
            pltpu.VMEM((INNER, 8, 128), F32),
            dma((7 + 2 * CHUNKS,)),
            dma((7 + 2 * CHUNKS,)),
            dma((tp_count,)),
            dma((tp_count,)),
            dma((INNER,)),
            dma((INNER,)),
            dma((outer,)),
            dma((outer,)),
            dma((INNER,)),
            dma((INNER,)),
            pltpu.VMEM((INNER, 16, 128), F32),
            pltpu.VMEM((outer, 16, 128), F32),
            tiled(24),
            dma((INNER,)),
            dma((INNER,)),
            dma((outer,)),
            dma((outer,)),
            pltpu.VMEM((length, width), BF16),
            pltpu.VMEM((length, width), BF16),
            pltpu.VMEM((length, width), BF16),
            pltpu.VMEM((length, width), BF16),
            dma((4,)),
        ],
        compiler_params=pltpu.CompilerParams(collective_id=0, has_side_effects=True),
        name="operator",
    )(
        lengths,
        q_input,
        k_input,
        v_input,
        resid,
        cotangent,
        jnp.transpose(short_filter, (0, 2, 1)),
        long_filter,
        skip.reshape(1, width),
        gain.reshape(1, width),
    )
    outs = pl.pallas_call(
        finish,
        out_shape=tuple(jax.ShapeDtypeStruct(out.shape, out.dtype) for out in outs),
        in_specs=[pl.BlockSpec(memory_space=pl.ANY)] * 8,
        out_specs=(pl.BlockSpec(memory_space=pl.ANY),) * 8,
        scratch_shapes=[pltpu.VMEM(out.shape, out.dtype) for out in outs] + [dma((8,)), dma((8,))],
        name="finish",
    )(*outs)
    return outs[:4] + (
        jnp.transpose(outs[4], (0, 2, 1)),
        outs[5],
        outs[6].reshape(width),
        outs[7].reshape(width),
    )


def solution(mesh):
    rows = P("ctx", "tp")
    return jax.shard_map(
        shards,
        mesh=mesh,
        in_specs=(
            rows,
            rows,
            rows,
            rows,
            P(),
            P(None, "tp", None),
            P("tp", None),
            P("tp"),
            P("tp"),
            rows,
        ),
        out_specs=(rows, rows, rows, rows, P(None, "tp", None), P("tp", None), P("tp"), P("tp")),
        check_vma=False,
    )
```

```python
import functools

import jax
import jax.numpy as jnp
from jax import lax
from jax.experimental import pallas as pl
from jax.experimental.pallas import tpu as pltpu
from jax.sharding import PartitionSpec as P

C = 4096
GS = 16
K = 128
KS = 7
EPS = 1e-06
INNER = 16
MESH_ID = pl.DeviceIdType.MESH
F32 = jnp.float32
BF16 = jnp.bfloat16
HIGH = lax.Precision.HIGHEST
RIM = 8
HEAD = 16
CHUNKS = 4


def iota(shape, axis):
    return lax.broadcasted_iota(jnp.int32, shape, axis)


def skewed(x):
    return pltpu.roll(x, 0, 1, stride=1, stride_axis=0)


def body(
    count,
    tp_count,
    lengths,
    q_ref,
    k_ref,
    v_ref,
    resid_hbm,
    cot_hbm,
    short_ref,
    long_ref,
    skip_ref,
    gain_ref,
    normed_out,
    gq_out,
    gk_out,
    gv_out,
    gshort_out,
    glong_out,
    gskip_out,
    ggain_out,
    tail_s,
    tail_r,
    tail2_r,
    headk_r,
    headv_r,
    head_s,
    head_r,
    gext,
    gmx,
    gqs_s,
    gqs_r,
    xq,
    xk,
    xv,
    pk,
    pv,
    sq,
    sk,
    sv,
    mixed_s,
    summed_s,
    eq,
    ek,
    ev,
    fmat,
    umat,
    xmat,
    mats,
    xmasks,
    taps_m,
    prev_m,
    taps_w,
    wfwd,
    wrev,
    glong_s,
    stats,
    xs,
    first,
    second,
    result,
    hs,
    hr,
    ts,
    tr,
    s1,
    r1,
    s2,
    r2,
    s3,
    r3,
    near_s,
    far_s,
    tsum,
    s4,
    r4,
    s5,
    r5,
    resid_ref,
    cot_ref,
    ls,
):
    length, width = q_ref.shape
    tiles = width // 128
    per = 128 // GS
    groups = width // GS
    ctx = lax.axis_index("ctx")
    tp = lax.axis_index("tp")
    outer = count // INNER
    hi = ctx // INNER
    lo = ctx % INNER
    total = count * length
    base = ctx * length

    def along(by):
        return (ctx + by + count) % count

    def inner_peer(k):
        return (lo + k) % INNER

    def outer_peer(k):
        return (hi + k) % outer

    def tp_peer(k):
        return (tp + k) % tp_count

    barrier = pltpu.get_barrier_semaphore()
    for by in (1, 2, -1, -2):
        pl.semaphore_signal(barrier, inc=1, device_id={"ctx": along(by)}, device_id_type=MESH_ID)
    for k in range(1, tp_count):
        pl.semaphore_signal(barrier, inc=1, device_id={"tp": tp_peer(k)}, device_id_type=MESH_ID)
    for k in range(1, INNER):
        pl.semaphore_signal(
            barrier, inc=1, device_id={"ctx": hi * INNER + inner_peer(k)}, device_id_type=MESH_ID
        )
    for k in range(1, outer):
        pl.semaphore_signal(
            barrier, inc=1, device_id={"ctx": outer_peer(k) * INNER + lo}, device_id_type=MESH_ID
        )

    def halo(slot, src, dst, by):
        return pltpu.make_async_remote_copy(
            src_ref=src,
            dst_ref=dst,
            send_sem=hs.at[slot],
            recv_sem=hr.at[slot],
            device_id={"ctx": along(by)},
            device_id_type=MESH_ID,
        )

    tails = halo(0, tail_s, tail_r, 1)
    tails2 = halo(1, tail_s.at[pl.ds(1, 2)], tail2_r, 2)
    heads_k = halo(2, k_ref.at[pl.ds(0, HEAD)], headk_r, 1)
    heads_v = halo(3, v_ref.at[pl.ds(0, HEAD)], headv_r, 1)
    heads_back = halo(4, head_s, head_r, -1)
    gm_far = halo(5, gmx.at[:, pl.ds(0, HEAD)], gmx.at[:, pl.ds(2 * K, HEAD)], -2)
    gqs_copy = halo(6, gqs_s, gqs_r, -1)
    each = tiles // CHUNKS
    gated_copies = []
    gm_copies = []
    for c in range(CHUNKS):
        some = pl.ds(c * each, each)
        gated_copies.append(
            halo(
                7 + c,
                gext.at[some, pl.ds(K + HEAD, K - HEAD)],
                gext.at[some, pl.ds(HEAD, K - HEAD)],
                1,
            )
        )
        gm_copies.append(
            halo(7 + CHUNKS + c, gmx.at[some, pl.ds(0, K)], gmx.at[some, pl.ds(K, K)], -1)
        )

    for s, ref in enumerate((q_ref, k_ref, v_ref)):
        tail_s[s] = ref[length - HEAD :, :].astype(F32)[HEAD - RIM :].astype(BF16)
    head_s[0] = k_ref[0:HEAD, :].astype(F32)[:RIM].astype(BF16)
    head_s[1] = v_ref[0:HEAD, :].astype(F32)[:RIM].astype(BF16)

    loads = [
        pltpu.make_async_copy(resid_hbm, resid_ref, ls.at[0]),
        pltpu.make_async_copy(cot_hbm, cot_ref, ls.at[1]),
    ]
    for load in loads:
        load.start()

    starts = []
    at = jnp.int32(0)
    for i in range(lengths.shape[0]):
        starts.append(at)
        at = at + lengths[i]

    def position(token):
        begin = jnp.zeros_like(token)
        for start in starts:
            begin = jnp.where(token >= start, start, begin)
        return token - begin

    def flag(cond):
        return jnp.where(cond, 1.0, 0.0).astype(F32)

    token = base - RIM + iota((length + 2 * RIM, 128), 0)
    pos = position(token)
    for j in range(KS):
        taps_m[j] = flag((pos >= j) & (token < total))
    picks = flag(iota((groups, width), 1) // GS == iota((groups, width), 0)).astype(BF16)
    for s in range(3):
        table = jnp.dot(short_ref[s], picks, preferred_element_type=F32)
        for t in range(tiles):
            taps_w[t, pl.ds(s * 8, KS), :] = table[:, t * 128 : (t + 1) * 128]

    def lanes(t):
        return pl.ds(pl.multiple_of(t * 128, 128), 128)

    def short_sum(buf, t, s, first_row, rows, mask, mask_row):
        result_sum = taps_w[t, pl.ds(s * 8, 1), :] * buf[t, pl.ds(RIM + first_row, rows), :]
        for j in range(1, KS):
            moved = buf[t, pl.ds(RIM + first_row - j, rows), :]
            result_sum = result_sum + taps_w[t, pl.ds(s * 8 + j, 1), :] * (
                moved * mask[j, pl.ds(mask_row, rows), :]
            )
        return result_sum

    rest = length - HEAD

    def gate_main(t, carry):
        xk[t, pl.ds(RIM, length), :] = k_ref[:, lanes(t)].astype(F32)
        xv[t, pl.ds(RIM, length), :] = v_ref[:, lanes(t)].astype(F32)
        ks = short_sum(xk, t, 1, HEAD, rest, taps_m, RIM + HEAD)
        vs = short_sum(xv, t, 2, HEAD, rest, taps_m, RIM + HEAD)
        sk[t, pl.ds(HEAD, rest), :] = ks
        sv[t, pl.ds(HEAD, rest), :] = vs
        gext[t, pl.ds(K + HEAD, rest), :] = (ks * vs).astype(BF16)
        return carry

    lax.fori_loop(0, tiles, gate_main, 0)
    pl.semaphore_wait(barrier, 4 + tp_count - 1 + INNER - 1 + outer - 1)
    tails.start()
    tails2.start()
    heads_k.start()
    heads_v.start()
    for copy in gated_copies:
        copy.start()
    heads_back.start()

    def query_main(t, carry):
        xq[t, pl.ds(RIM, length), :] = q_ref[:, lanes(t)].astype(F32)
        sq[t, pl.ds(HEAD, rest), :] = short_sum(xq, t, 0, HEAD, rest, taps_m, RIM + HEAD)
        return carry

    lax.fori_loop(0, tiles, query_main, 0)

    token = base - K + iota((HEAD, 128), 0)
    pos = position(token)
    for j in range(KS):
        prev_m[j] = flag(pos >= j)
    row = iota((K, 128), 0)
    col = iota((K, 128), 1)
    pos = position(base + row)
    mats[0] = flag((col > row) & (pos >= row - col + K))
    mats[1] = flag((col <= row) & (pos >= row - col))
    pos = position(base + col)
    mats[2] = flag((col >= row) & (pos >= col - row))
    token = base + K + col
    pos = position(token)
    mats[3] = flag((col < row) & (pos >= K + col - row) & (token < total))
    near_row = iota((8, 128), 0)
    near_col = iota((8, 128), 1)
    token = base + K + near_col
    pos = position(token)
    xmasks[0] = flag((near_col >= near_row) & (pos >= near_col - near_row) & (token < total))
    token = token + K
    pos = position(token)
    xmasks[1] = flag((near_col < near_row) & (pos >= K + near_col - near_row) & (token < total))

    flip = flag((row + col) % K == 0)
    wfwd[...] = long_ref[...].astype(F32)
    wrev[...] = jnp.dot(long_ref[...], flip.astype(BF16), preferred_element_type=F32)

    def build(t, carry):
        forward = wfwd[pl.ds(pl.multiple_of(t * per, per), per), :]
        backward = wrev[pl.ds(pl.multiple_of(t * per, per), per), :]
        extra = []
        for g in range(per):
            band = skewed(jnp.broadcast_to(backward[g : g + 1, :], (K, K)))
            fmat[t, pl.ds(g * K, K), pl.ds(0, K)] = (band * mats[0]).astype(BF16)
            fmat[t, pl.ds(g * K, K), pl.ds(K, K)] = (band * mats[1]).astype(BF16)
            band = skewed(jnp.broadcast_to(forward[g : g + 1, :], (K, K)))
            umat[t, pl.ds(g * K, K), pl.ds(0, K)] = (band * mats[2]).astype(BF16)
            umat[t, pl.ds(g * K, K), pl.ds(K, K)] = (band * mats[3]).astype(BF16)
            near = band[0:8, :]
            extra.append(jnp.concatenate([near * xmasks[0], near * xmasks[1]], axis=1))
        xmat[t] = jnp.concatenate(extra, axis=0).astype(BF16)
        return carry

    lax.fori_loop(0, tiles, build, 0)
    gmx[:, pl.ds(2 * K + HEAD, K - HEAD), :] = jnp.zeros((tiles, K - HEAD, 128), BF16)

    tails.wait_recv()
    tails2.wait_recv()
    heads_k.wait_recv()
    heads_v.wait_recv()
    for t in range(tiles):
        part = slice(t * 128, (t + 1) * 128)
        for s, buf in enumerate((xq, xk, xv)):
            buf[t, pl.ds(0, RIM), :] = tail_r[s, :, part].astype(F32)
        for s, (buf, prev, head) in enumerate(((xk, pk, headk_r), (xv, pv, headv_r))):
            prev[t, pl.ds(0, RIM), :] = tail2_r[s, :, part].astype(F32)
            prev[t, pl.ds(RIM, HEAD), :] = head[:, part].astype(F32)

    def gate_rims(t, carry):
        sq[t, pl.ds(0, HEAD), :] = short_sum(xq, t, 0, 0, HEAD, taps_m, RIM)
        ks = short_sum(xk, t, 1, 0, HEAD, taps_m, RIM)
        vs = short_sum(xv, t, 2, 0, HEAD, taps_m, RIM)
        sk[t, pl.ds(0, HEAD), :] = ks
        sv[t, pl.ds(0, HEAD), :] = vs
        gext[t, pl.ds(K, HEAD), :] = (ks * vs).astype(BF16)
        ks = short_sum(pk, t, 1, 0, HEAD, prev_m, 0)
        vs = short_sum(pv, t, 2, 0, HEAD, prev_m, 0)
        gext[t, pl.ds(0, HEAD), :] = (ks * vs).astype(BF16)
        return carry

    lax.fori_loop(0, tiles, gate_rims, 0)

    def select(products, rows):
        group = iota((rows, 128), 1) // GS
        picked = products[0:rows]
        for g in range(1, per):
            picked = jnp.where(group == g, products[g * rows : (g + 1) * rows], picked)
        return picked

    def mix(t, carry):
        squares, products = carry
        source = gext[t]
        conv = select(jnp.dot(fmat[t], source, preferred_element_type=F32), K)
        gated = gext[t, pl.ds(K, K), :].astype(F32)
        mixed = conv + skip_ref[:, lanes(t)] * gated
        summed = resid_ref[:, lanes(t)].astype(F32) + sq[t] * mixed
        mixed_s[t] = mixed
        summed_s[t] = summed
        squares = squares + summed * summed
        products = products + gain_ref[:, lanes(t)] * cot_ref[:, lanes(t)].astype(F32) * summed
        return squares, products

    for load in loads:
        load.wait()
    zero = jnp.zeros((length, 128), F32)
    squares, products = zero, zero
    for c in range(CHUNKS):
        gated_copies[c].wait_recv()
        squares, products = lax.fori_loop(c * each, (c + 1) * each, mix, (squares, products))
    squares = jnp.sum(squares.T, axis=0, keepdims=True)
    products = jnp.sum(products.T, axis=0, keepdims=True)
    stats[tp] = jnp.where(near_row == 0, squares, products)

    def share(k):
        return pltpu.make_async_remote_copy(
            src_ref=stats.at[tp],
            dst_ref=stats.at[tp],
            send_sem=ts.at[k],
            recv_sem=tr.at[tp],
            device_id={"tp": tp_peer(k)},
            device_id_type=MESH_ID,
        )

    def arrived(sem, buf, slot):
        pltpu.make_async_copy(buf.at[slot], buf.at[slot], sem.at[slot]).wait()

    for k in range(1, tp_count):
        share(k).start()
    for k in range(1, tp_count):
        arrived(tr, stats, tp_peer(tp_count - k))
    both = stats[0]
    for i in range(1, tp_count):
        both = both + stats[i]
    both = both / (width * tp_count)
    shifted = both[0:1] + EPS
    inverse_row = lax.rsqrt(shifted)
    inverse_row = inverse_row * (1.5 - 0.5 * shifted * inverse_row * inverse_row)
    pull_row = inverse_row * inverse_row * both[1:2]
    inverse = jnp.broadcast_to(inverse_row, (128, length)).T
    pull = jnp.broadcast_to(pull_row, (128, length)).T
    mats[4] = inverse
    mats[5] = pull

    def grads(t, carry):
        inverse = mats[4]
        summed = summed_s[t]
        gain = gain_ref[:, lanes(t)]
        cot = cot_ref[:, lanes(t)].astype(F32)
        normed_out[:, lanes(t)] = (gain * summed * inverse).astype(BF16)
        grad_sum = inverse * (gain * cot - summed * mats[5])
        grad_mixed = (grad_sum * sq[t]).astype(BF16)
        gmx[t, pl.ds(0, K), :] = grad_mixed
        grad_qs = (grad_sum * mixed_s[t]).astype(BF16)
        eq[t, pl.ds(0, length), :] = grad_qs.astype(F32)
        gqs_s[:, lanes(t)] = grad_qs.astype(F32)[:RIM].astype(BF16)
        gated = gext[t, pl.ds(K, K), :].astype(F32)
        xs[8, pl.ds(t, 1), :] = jnp.sum(grad_mixed.astype(F32) * gated, axis=0, keepdims=True)
        xs[9, pl.ds(t, 1), :] = jnp.sum(cot * summed * inverse, axis=0, keepdims=True)
        return carry

    lax.fori_loop(0, tiles, grads, 0)
    gqs_copy.start()
    gm_far.start()
    for copy in gm_copies:
        copy.start()

    def correlate(t, carry):
        grad_mixed = gmx[t, pl.ds(0, K), :]
        source = gext[t]
        group = iota((K, 128), 1) // GS
        left = jnp.concatenate(
            [jnp.where(group == g, grad_mixed, jnp.zeros_like(grad_mixed)) for g in range(per)], axis=0
        )
        cross = lax.dot_general(
            left, source, (((1,), (1,)), ((), ())), preferred_element_type=F32
        )
        for g in range(per):
            block = cross[g * K : (g + 1) * K]
            band = block[:, :K] * mats[0] + block[:, K:] * mats[1]
            folded = band[0:8]
            for a in range(1, K // 8):
                folded = folded + pltpu.roll(band[a * 8 : (a + 1) * 8], K - a * 8, 1)
            glong_s[pl.ds(pl.multiple_of(t * per * 8, 8) + g * 8, 8), :] = folded
        return carry

    lax.fori_loop(0, tiles, correlate, 0)
    folded = glong_s[pl.ds(0, groups, stride=8), :]
    for b in range(1, 8):
        folded = folded + pltpu.roll(glong_s[pl.ds(b, groups, stride=8), :], K - b, 1)
    turned = jnp.dot(folded, flip, precision=HIGH, preferred_element_type=F32)
    for t in range(tiles):
        xs[t] = turned[t * per : (t + 1) * per]
    for i in range(10, INNER):
        xs[i] = jnp.zeros((8, 128), F32)
    tsum[...] = jnp.zeros_like(tsum)

    def copy_to(src, dst, send, recv, device):
        return pltpu.make_async_remote_copy(
            src_ref=src,
            dst_ref=dst,
            send_sem=send,
            recv_sem=recv,
            device_id={"ctx": device},
            device_id_type=MESH_ID,
        )

    def inner_device(k):
        return hi * INNER + inner_peer(k)

    def outer_device(k):
        return outer_peer(k) * INNER + lo

    def scatter(k):
        return copy_to(xs.at[inner_peer(k)], first.at[lo], s1.at[k], r1.at[lo], inner_device(k))

    def exchange(k):
        return copy_to(second.at[hi], second.at[hi], s2.at[k], r2.at[hi], outer_device(k))

    def gather(k):
        return copy_to(result.at[lo], result.at[lo], s3.at[k], r3.at[lo], inner_device(k))

    def near_sums(k):
        return copy_to(near_s.at[lo], near_s.at[lo], s4.at[k], r4.at[lo], inner_device(k))

    def far_sums(k):
        return copy_to(far_s.at[hi], far_s.at[hi], s5.at[k], r5.at[hi], outer_device(k))

    for k in range(1, INNER):
        scatter(k).start()

    heads_back.wait_recv()

    def gate_next(t, carry):
        for s, buf in enumerate((xk, xv)):
            buf[t, pl.ds(RIM + length, RIM), :] = head_r[s, :, lanes(t)].astype(F32)
        sk[t, pl.ds(length, RIM), :] = short_sum(xk, t, 1, length, RIM, taps_m, RIM + length)
        sv[t, pl.ds(length, RIM), :] = short_sum(xv, t, 2, length, RIM, taps_m, RIM + length)
        return carry

    lax.fori_loop(0, tiles, gate_next, 0)
    gqs_copy.wait_recv()
    gm_far.wait_recv()

    def rounded(value):
        return value.astype(BF16).astype(F32)

    def back(t, carry):
        conv = select(
            jnp.dot(umat[t], gmx[t, pl.ds(0, 2 * K), :], preferred_element_type=F32), K
        )
        extra = select(
            jnp.dot(xmat[t], gmx[t, pl.ds(K, 2 * K), :], preferred_element_type=F32), 8
        )
        skip = skip_ref[:, lanes(t)]
        grad_gated = skip * gmx[t, pl.ds(0, K), :].astype(F32) + conv
        ek[t, pl.ds(0, length), :] = rounded(grad_gated * sv[t, pl.ds(0, length), :])
        ev[t, pl.ds(0, length), :] = rounded(grad_gated * sk[t, pl.ds(0, length), :])
        near = gmx[t, pl.ds(K, HEAD), :].astype(F32)[:RIM]
        grad_gated = skip * near + extra
        ek[t, pl.ds(length, RIM), :] = rounded(grad_gated * sv[t, pl.ds(length, RIM), :])
        ev[t, pl.ds(length, RIM), :] = rounded(grad_gated * sk[t, pl.ds(length, RIM), :])
        eq[t, pl.ds(length, RIM), :] = gqs_r[:, lanes(t)].astype(F32)
        for s, (buf, values) in enumerate(((eq, xq), (ek, xk), (ev, xv))):
            own = values[t, pl.ds(RIM, length), :]
            for j in range(KS):
                moved = buf[t, pl.ds(j, length), :] * taps_m[j, pl.ds(RIM + j, length), :]
                tsum[t, pl.ds(s * 8 + j, 1), :] = jnp.sum(moved * own, axis=0, keepdims=True)
        return carry

    for c in range(CHUNKS):
        gm_copies[c].wait_recv()
        lax.fori_loop(c * each, (c + 1) * each, back, 0)
    spread_sums = jnp.zeros((72, 128), F32)
    for t in range(tiles):
        sums = tsum[t]
        high = sums.astype(BF16).astype(F32)
        middle = (sums - high).astype(BF16).astype(F32)
        parts = jnp.concatenate([high, middle, sums - high - middle], axis=0).astype(BF16)
        spread = flag(row // GS + t * per == col).astype(BF16)
        spread_sums = spread_sums + jnp.dot(parts, spread, preferred_element_type=F32)
    spread_sums = spread_sums[0:24] + spread_sums[24:48] + spread_sums[48:72]
    near_s[lo, pl.ds(0, 8), :] = spread_sums[0:8] + pltpu.roll(spread_sums[8:16], 64, 1)
    near_s[lo, pl.ds(8, 8), :] = spread_sums[16:24]
    for k in range(1, INNER):
        near_sums(k).start()
    sums = xs[lo]
    for k in range(1, INNER):
        slot = inner_peer(INNER - k)
        arrived(r1, first, slot)
        sums = sums + first[slot]
    second[hi] = sums
    for k in range(1, outer):
        exchange(k).start()

    def streams(t, carry):
        for s, (buf, out) in enumerate(((eq, gq_out), (ek, gk_out), (ev, gv_out))):
            result_sum = jnp.zeros((length, 128), F32)
            for j in range(KS):
                moved = buf[t, pl.ds(j, length), :] * taps_m[j, pl.ds(RIM + j, length), :]
                result_sum = result_sum + taps_w[t, pl.ds(s * 8 + j, 1), :] * moved
            out[:, lanes(t)] = result_sum.astype(BF16)
        return carry

    lax.fori_loop(0, tiles, streams, 0)

    for k in range(1, outer):
        arrived(r2, second, outer_peer(outer - k))
    sums = second[0]
    for i in range(1, outer):
        sums = sums + second[i]
    result[lo] = sums
    for k in range(1, INNER):
        gather(k).start()

    for k in range(1, INNER):
        arrived(r4, near_s, inner_peer(INNER - k))
    sums = near_s[0]
    for i in range(1, INNER):
        sums = sums + near_s[i]
    far_s[hi] = sums
    for k in range(1, outer):
        far_sums(k).start()

    for k in range(1, INNER):
        arrived(r3, result, inner_peer(INNER - k))
    for t in range(tiles):
        glong_out[pl.ds(t * per, per), :] = result[t]
    gskip_out[...] = result[8]
    ggain_out[...] = result[9]
    for copy in [tails, tails2, heads_k, heads_v, heads_back, gm_far, gqs_copy] + gated_copies + gm_copies:
        copy.wait_send()
    for k in range(1, tp_count):
        share(k).wait_send()
    for k in range(1, INNER):
        scatter(k).wait_send()
        gather(k).wait_send()
        near_sums(k).wait_send()
    for k in range(1, outer):
        exchange(k).wait_send()

    for k in range(1, outer):
        arrived(r5, far_s, outer_peer(outer - k))
    sums = far_s[0]
    for i in range(1, outer):
        sums = sums + far_s[i]
    gshort_out[0] = sums[:KS, :groups]
    gshort_out[1] = sums[:KS, 64 : 64 + groups]
    gshort_out[2] = sums[8 : 8 + KS, :groups]
    for k in range(1, outer):
        far_sums(k).wait_send()


def finish(*refs):
    half = (len(refs) - 1) // 2
    left = refs[-1]
    copies = [pltpu.make_async_copy(refs[i], refs[half + i], left.at[i]) for i in range(half)]
    for copy in copies:
        copy.start()
    for copy in copies:
        copy.wait()


def shards(
    q_input, k_input, v_input, resid, lengths, short_filter, long_filter, skip, gain, cotangent
):
    length, width = q_input.shape
    tiles = width // 128
    groups = width // GS
    per = 128 // GS
    count = lax.axis_size("ctx")
    tp_count = lax.axis_size("tp")
    outer = count // INNER
    vmem = pl.BlockSpec(memory_space=pltpu.VMEM)
    large = pltpu.VMEM((length, width), BF16)

    def tiled(rows):
        return pltpu.VMEM((tiles, rows, 128), F32)

    dma = pltpu.SemaphoreType.DMA
    outs = pl.pallas_call(
        functools.partial(body, count, tp_count),
        out_shape=(
            large,
            large,
            large,
            large,
            pltpu.VMEM((3, KS, groups), F32),
            pltpu.VMEM((groups, K), F32),
            pltpu.VMEM((tiles, 128), F32),
            pltpu.VMEM((tiles, 128), F32),
        ),
        in_specs=[pl.BlockSpec(memory_space=pltpu.SMEM)] + [vmem] * 3 + [pl.BlockSpec(memory_space=pl.ANY)] * 2 + [vmem] * 4,
        out_specs=(vmem,) * 8,
        scratch_shapes=[
            pltpu.VMEM((3, RIM, width), BF16),
            pltpu.VMEM((3, RIM, width), BF16),
            pltpu.VMEM((2, RIM, width), BF16),
            pltpu.VMEM((HEAD, width), BF16),
            pltpu.VMEM((HEAD, width), BF16),
            pltpu.VMEM((2, RIM, width), BF16),
            pltpu.VMEM((2, RIM, width), BF16),
            pltpu.VMEM((tiles, 2 * K, 128), BF16),
            pltpu.VMEM((tiles, 3 * K, 128), BF16),
            pltpu.VMEM((RIM, width), BF16),
            pltpu.VMEM((RIM, width), BF16),
            tiled(length + 2 * RIM),
            tiled(length + 2 * RIM),
            tiled(length + 2 * RIM),
            tiled(RIM + HEAD),
            tiled(RIM + HEAD),
            tiled(length),
            tiled(length + RIM),
            tiled(length + RIM),
            tiled(length),
            tiled(length),
            tiled(length + RIM),
            tiled(length + RIM),
            tiled(length + RIM),
            pltpu.VMEM((tiles, per * K, 2 * K), BF16),
            pltpu.VMEM((tiles, per * K, 2 * K), BF16),
            pltpu.VMEM((tiles, per * 8, 2 * K), BF16),
            pltpu.VMEM((6, K, 128), F32),
            pltpu.VMEM((2, 8, 128), F32),
            pltpu.VMEM((KS, length + 2 * RIM, 128), F32),
            pltpu.VMEM((KS, HEAD, 128), F32),
            tiled(24),
            pltpu.VMEM((groups, K), F32),
            pltpu.VMEM((groups, K), F32),
            pltpu.VMEM((groups * 8, K), F32),
            pltpu.VMEM((tp_count, 8, 128), F32),
            pltpu.VMEM((INNER, 8, 128), F32),
            pltpu.VMEM((INNER, 8, 128), F32),
            pltpu.VMEM((outer, 8, 128), F32),
            pltpu.VMEM((INNER, 8, 128), F32),
            dma((7 + 2 * CHUNKS,)),
            dma((7 + 2 * CHUNKS,)),
            dma((tp_count,)),
            dma((tp_count,)),
            dma((INNER,)),
            dma((INNER,)),
            dma((outer,)),
            dma((outer,)),
            dma((INNER,)),
            dma((INNER,)),
            pltpu.VMEM((INNER, 16, 128), F32),
            pltpu.VMEM((outer, 16, 128), F32),
            tiled(24),
            dma((INNER,)),
            dma((INNER,)),
            dma((outer,)),
            dma((outer,)),
            pltpu.VMEM((length, width), BF16),
            pltpu.VMEM((length, width), BF16),
            dma((2,)),
        ],
        compiler_params=pltpu.CompilerParams(collective_id=0, has_side_effects=True),
        name="operator",
    )(
        lengths,
        q_input,
        k_input,
        v_input,
        resid,
        cotangent,
        jnp.transpose(short_filter, (0, 2, 1)),
        long_filter,
        skip.reshape(1, width),
        gain.reshape(1, width),
    )
    outs = pl.pallas_call(
        finish,
        out_shape=tuple(jax.ShapeDtypeStruct(out.shape, out.dtype) for out in outs),
        in_specs=[vmem] * 8,
        out_specs=(pl.BlockSpec(memory_space=pl.ANY),) * 8,
        scratch_shapes=[dma((8,))],
        name="finish",
    )(*[pltpu.with_memory_space_constraint(out, pltpu.VMEM) for out in outs])
    return outs[:4] + (
        jnp.transpose(outs[4], (0, 2, 1)),
        outs[5],
        outs[6].reshape(width),
        outs[7].reshape(width),
    )


def solution(mesh):
    rows = P("ctx", "tp")
    return jax.shard_map(
        shards,
        mesh=mesh,
        in_specs=(
            rows,
            rows,
            rows,
            rows,
            P(),
            P(None, "tp", None),
            P("tp", None),
            P("tp"),
            P("tp"),
            rows,
        ),
        out_specs=(rows, rows, rows, rows, P(None, "tp", None), P("tp", None), P("tp"), P("tp")),
        check_vma=False,
    )
```

```python
import functools

import jax
import jax.numpy as jnp
from jax import lax
from jax.experimental import pallas as pl
from jax.experimental.pallas import tpu as pltpu
from jax.sharding import PartitionSpec as P

C = 4096
GS = 16
K = 128
KS = 7
EPS = 1e-06
INNER = 16
MESH_ID = pl.DeviceIdType.MESH
F32 = jnp.float32
BF16 = jnp.bfloat16
HIGH = lax.Precision.HIGHEST
RIM = 8
HEAD = 16
CHUNKS = 4


def far_first(ring):
    return sorted(range(1, ring), key=lambda k: -min(k, ring - k))


def iota(shape, axis):
    return lax.broadcasted_iota(jnp.int32, shape, axis)


def skewed(x):
    return pltpu.roll(x, 0, 1, stride=1, stride_axis=0)


def body(
    count,
    tp_count,
    lengths,
    q_ref,
    k_ref,
    v_ref,
    resid_hbm,
    cot_hbm,
    short_ref,
    long_ref,
    skip_ref,
    gain_ref,
    normed_out,
    gq_out,
    gk_out,
    gv_out,
    gshort_out,
    glong_out,
    gskip_out,
    ggain_out,
    tail_s,
    tail_r,
    tail2_r,
    headk_r,
    headv_r,
    head_s,
    head_r,
    gext,
    gmx,
    gqs_s,
    gqs_r,
    xq,
    xk,
    xv,
    pk,
    pv,
    sq,
    sk,
    sv,
    mixed_s,
    summed_s,
    eq,
    ek,
    ev,
    fmat,
    umat,
    xmat,
    mats,
    xmasks,
    taps_m,
    prev_m,
    taps_w,
    wfwd,
    wrev,
    glong_s,
    stats,
    xs,
    first,
    second,
    result,
    hs,
    hr,
    ts,
    tr,
    s1,
    r1,
    s2,
    r2,
    s3,
    r3,
    near_s,
    far_s,
    tsum,
    s4,
    r4,
    s5,
    r5,
    resid_ref,
    cot_ref,
    ls,
):
    length, width = q_ref.shape
    tiles = width // 128
    per = 128 // GS
    groups = width // GS
    ctx = lax.axis_index("ctx")
    tp = lax.axis_index("tp")
    outer = count // INNER
    hi = ctx // INNER
    lo = ctx % INNER
    total = count * length
    base = ctx * length

    def along(by):
        return (ctx + by + count) % count

    def inner_peer(k):
        return (lo + k) % INNER

    def outer_peer(k):
        return (hi + k) % outer

    def tp_peer(k):
        return (tp + k) % tp_count

    barrier = pltpu.get_barrier_semaphore()
    for by in (1, 2, -1, -2):
        pl.semaphore_signal(barrier, inc=1, device_id={"ctx": along(by)}, device_id_type=MESH_ID)
    for k in range(1, tp_count):
        pl.semaphore_signal(barrier, inc=1, device_id={"tp": tp_peer(k)}, device_id_type=MESH_ID)
    for k in range(1, INNER):
        pl.semaphore_signal(
            barrier, inc=1, device_id={"ctx": hi * INNER + inner_peer(k)}, device_id_type=MESH_ID
        )
    for k in range(1, outer):
        pl.semaphore_signal(
            barrier, inc=1, device_id={"ctx": outer_peer(k) * INNER + lo}, device_id_type=MESH_ID
        )

    def halo(slot, src, dst, by):
        return pltpu.make_async_remote_copy(
            src_ref=src,
            dst_ref=dst,
            send_sem=hs.at[slot],
            recv_sem=hr.at[slot],
            device_id={"ctx": along(by)},
            device_id_type=MESH_ID,
        )

    tails = halo(0, tail_s, tail_r, 1)
    tails2 = halo(1, tail_s.at[pl.ds(1, 2)], tail2_r, 2)
    heads_k = halo(2, k_ref.at[pl.ds(0, HEAD)], headk_r, 1)
    heads_v = halo(3, v_ref.at[pl.ds(0, HEAD)], headv_r, 1)
    heads_back = halo(4, head_s, head_r, -1)
    gm_far = halo(5, gmx.at[:, pl.ds(0, HEAD)], gmx.at[:, pl.ds(2 * K, HEAD)], -2)
    gqs_copy = halo(6, gqs_s, gqs_r, -1)
    each = tiles // CHUNKS
    gated_copies = []
    gm_copies = []
    for c in range(CHUNKS):
        some = pl.ds(c * each, each)
        gated_copies.append(
            halo(
                7 + c,
                gext.at[some, pl.ds(K + HEAD, K - HEAD)],
                gext.at[some, pl.ds(HEAD, K - HEAD)],
                1,
            )
        )
        gm_copies.append(
            halo(7 + CHUNKS + c, gmx.at[some, pl.ds(0, K)], gmx.at[some, pl.ds(K, K)], -1)
        )

    for s, ref in enumerate((q_ref, k_ref, v_ref)):
        tail_s[s] = ref[length - HEAD :, :].astype(F32)[HEAD - RIM :].astype(BF16)
    head_s[0] = k_ref[0:HEAD, :].astype(F32)[:RIM].astype(BF16)
    head_s[1] = v_ref[0:HEAD, :].astype(F32)[:RIM].astype(BF16)

    loads = [
        pltpu.make_async_copy(resid_hbm, resid_ref, ls.at[0]),
        pltpu.make_async_copy(cot_hbm, cot_ref, ls.at[1]),
    ]
    for load in loads:
        load.start()

    starts = []
    at = jnp.int32(0)
    for i in range(lengths.shape[0]):
        starts.append(at)
        at = at + lengths[i]

    def position(token):
        begin = jnp.zeros_like(token)
        for start in starts:
            begin = jnp.where(token >= start, start, begin)
        return token - begin

    def flag(cond):
        return jnp.where(cond, 1.0, 0.0).astype(F32)

    token = base - RIM + iota((length + 2 * RIM, 128), 0)
    pos = position(token)
    for j in range(KS):
        taps_m[j] = flag((pos >= j) & (token < total))
    picks = flag(iota((groups, width), 1) // GS == iota((groups, width), 0)).astype(BF16)
    for s in range(3):
        table = jnp.dot(short_ref[s], picks, preferred_element_type=F32)
        for t in range(tiles):
            taps_w[t, pl.ds(s * 8, KS), :] = table[:, t * 128 : (t + 1) * 128]

    def lanes(t):
        return pl.ds(pl.multiple_of(t * 128, 128), 128)

    def short_sum(buf, t, s, first_row, rows, mask, mask_row):
        result_sum = taps_w[t, pl.ds(s * 8, 1), :] * buf[t, pl.ds(RIM + first_row, rows), :]
        for j in range(1, KS):
            moved = buf[t, pl.ds(RIM + first_row - j, rows), :]
            result_sum = result_sum + taps_w[t, pl.ds(s * 8 + j, 1), :] * (
                moved * mask[j, pl.ds(mask_row, rows), :]
            )
        return result_sum

    rest = length - HEAD

    def gate_main(t, carry):
        xk[t, pl.ds(RIM, length), :] = k_ref[:, lanes(t)].astype(F32)
        xv[t, pl.ds(RIM, length), :] = v_ref[:, lanes(t)].astype(F32)
        ks = short_sum(xk, t, 1, HEAD, rest, taps_m, RIM + HEAD)
        vs = short_sum(xv, t, 2, HEAD, rest, taps_m, RIM + HEAD)
        sk[t, pl.ds(HEAD, rest), :] = ks
        sv[t, pl.ds(HEAD, rest), :] = vs
        gext[t, pl.ds(K + HEAD, rest), :] = (ks * vs).astype(BF16)
        return carry

    lax.fori_loop(0, tiles, gate_main, 0)
    pl.semaphore_wait(barrier, 4 + tp_count - 1 + INNER - 1 + outer - 1)
    tails.start()
    tails2.start()
    heads_k.start()
    heads_v.start()
    for copy in gated_copies:
        copy.start()
    heads_back.start()

    def query_main(t, carry):
        xq[t, pl.ds(RIM, length), :] = q_ref[:, lanes(t)].astype(F32)
        sq[t, pl.ds(HEAD, rest), :] = short_sum(xq, t, 0, HEAD, rest, taps_m, RIM + HEAD)
        return carry

    lax.fori_loop(0, tiles, query_main, 0)

    token = base - K + iota((HEAD, 128), 0)
    pos = position(token)
    for j in range(KS):
        prev_m[j] = flag(pos >= j)
    row = iota((K, 128), 0)
    col = iota((K, 128), 1)
    pos = position(base + row)
    mats[0] = flag((col > row) & (pos >= row - col + K))
    mats[1] = flag((col <= row) & (pos >= row - col))
    pos = position(base + col)
    mats[2] = flag((col >= row) & (pos >= col - row))
    token = base + K + col
    pos = position(token)
    mats[3] = flag((col < row) & (pos >= K + col - row) & (token < total))
    near_row = iota((8, 128), 0)
    near_col = iota((8, 128), 1)
    token = base + K + near_col
    pos = position(token)
    xmasks[0] = flag((near_col >= near_row) & (pos >= near_col - near_row) & (token < total))
    token = token + K
    pos = position(token)
    xmasks[1] = flag((near_col < near_row) & (pos >= K + near_col - near_row) & (token < total))

    flip = flag((row + col) % K == 0)
    wfwd[...] = long_ref[...].astype(F32)
    wrev[...] = jnp.dot(long_ref[...], flip.astype(BF16), preferred_element_type=F32)

    def build(t, carry):
        forward = wfwd[pl.ds(pl.multiple_of(t * per, per), per), :]
        backward = wrev[pl.ds(pl.multiple_of(t * per, per), per), :]
        extra = []
        for g in range(per):
            band = skewed(jnp.broadcast_to(backward[g : g + 1, :], (K, K)))
            fmat[t, pl.ds(g * K, K), pl.ds(0, K)] = (band * mats[0]).astype(BF16)
            fmat[t, pl.ds(g * K, K), pl.ds(K, K)] = (band * mats[1]).astype(BF16)
            band = skewed(jnp.broadcast_to(forward[g : g + 1, :], (K, K)))
            umat[t, pl.ds(g * K, K), pl.ds(0, K)] = (band * mats[2]).astype(BF16)
            umat[t, pl.ds(g * K, K), pl.ds(K, K)] = (band * mats[3]).astype(BF16)
            near = band[0:8, :]
            extra.append(jnp.concatenate([near * xmasks[0], near * xmasks[1]], axis=1))
        xmat[t] = jnp.concatenate(extra, axis=0).astype(BF16)
        return carry

    lax.fori_loop(0, tiles, build, 0)
    gmx[:, pl.ds(2 * K + HEAD, K - HEAD), :] = jnp.zeros((tiles, K - HEAD, 128), BF16)

    tails.wait_recv()
    tails2.wait_recv()
    heads_k.wait_recv()
    heads_v.wait_recv()
    for t in range(tiles):
        part = slice(t * 128, (t + 1) * 128)
        for s, buf in enumerate((xq, xk, xv)):
            buf[t, pl.ds(0, RIM), :] = tail_r[s, :, part].astype(F32)
        for s, (buf, prev, head) in enumerate(((xk, pk, headk_r), (xv, pv, headv_r))):
            prev[t, pl.ds(0, RIM), :] = tail2_r[s, :, part].astype(F32)
            prev[t, pl.ds(RIM, HEAD), :] = head[:, part].astype(F32)

    def gate_rims(t, carry):
        sq[t, pl.ds(0, HEAD), :] = short_sum(xq, t, 0, 0, HEAD, taps_m, RIM)
        ks = short_sum(xk, t, 1, 0, HEAD, taps_m, RIM)
        vs = short_sum(xv, t, 2, 0, HEAD, taps_m, RIM)
        sk[t, pl.ds(0, HEAD), :] = ks
        sv[t, pl.ds(0, HEAD), :] = vs
        gext[t, pl.ds(K, HEAD), :] = (ks * vs).astype(BF16)
        ks = short_sum(pk, t, 1, 0, HEAD, prev_m, 0)
        vs = short_sum(pv, t, 2, 0, HEAD, prev_m, 0)
        gext[t, pl.ds(0, HEAD), :] = (ks * vs).astype(BF16)
        return carry

    lax.fori_loop(0, tiles, gate_rims, 0)

    def select(products, rows):
        group = iota((rows, 128), 1) // GS
        picked = products[0:rows]
        for g in range(1, per):
            picked = jnp.where(group == g, products[g * rows : (g + 1) * rows], picked)
        return picked

    def mix(t, carry):
        squares, products = carry
        source = gext[t]
        conv = select(jnp.dot(fmat[t], source, preferred_element_type=F32), K)
        gated = gext[t, pl.ds(K, K), :].astype(F32)
        mixed = conv + skip_ref[:, lanes(t)] * gated
        summed = resid_ref[:, lanes(t)].astype(F32) + sq[t] * mixed
        mixed_s[t] = mixed
        summed_s[t] = summed
        squares = squares + summed * summed
        products = products + gain_ref[:, lanes(t)] * cot_ref[:, lanes(t)].astype(F32) * summed
        return squares, products

    for load in loads:
        load.wait()
    zero = jnp.zeros((length, 128), F32)
    squares, products = zero, zero
    for c in range(CHUNKS):
        gated_copies[c].wait_recv()
        squares, products = lax.fori_loop(c * each, (c + 1) * each, mix, (squares, products))
    squares = jnp.sum(squares.T, axis=0, keepdims=True)
    products = jnp.sum(products.T, axis=0, keepdims=True)
    stats[tp] = jnp.where(near_row == 0, squares, products)

    def share(k):
        return pltpu.make_async_remote_copy(
            src_ref=stats.at[tp],
            dst_ref=stats.at[tp],
            send_sem=ts.at[k],
            recv_sem=tr.at[tp],
            device_id={"tp": tp_peer(k)},
            device_id_type=MESH_ID,
        )

    def arrived(sem, buf, slot):
        pltpu.make_async_copy(buf.at[slot], buf.at[slot], sem.at[slot]).wait()

    for k in range(1, tp_count):
        share(k).start()
    for k in range(1, tp_count):
        arrived(tr, stats, tp_peer(tp_count - k))
    both = stats[0]
    for i in range(1, tp_count):
        both = both + stats[i]
    both = both / (width * tp_count)
    shifted = both[0:1] + EPS
    inverse_row = lax.rsqrt(shifted)
    inverse_row = inverse_row * (1.5 - 0.5 * shifted * inverse_row * inverse_row)
    pull_row = inverse_row * inverse_row * both[1:2]
    inverse = jnp.broadcast_to(inverse_row, (128, length)).T
    pull = jnp.broadcast_to(pull_row, (128, length)).T
    mats[4] = inverse
    mats[5] = pull

    def grads(t, carry):
        inverse = mats[4]
        summed = summed_s[t]
        gain = gain_ref[:, lanes(t)]
        cot = cot_ref[:, lanes(t)].astype(F32)
        normed_out[:, lanes(t)] = (gain * summed * inverse).astype(BF16)
        grad_sum = inverse * (gain * cot - summed * mats[5])
        grad_mixed = (grad_sum * sq[t]).astype(BF16)
        gmx[t, pl.ds(0, K), :] = grad_mixed
        grad_qs = (grad_sum * mixed_s[t]).astype(BF16)
        eq[t, pl.ds(0, length), :] = grad_qs.astype(F32)
        gqs_s[:, lanes(t)] = grad_qs.astype(F32)[:RIM].astype(BF16)
        gated = gext[t, pl.ds(K, K), :].astype(F32)
        xs[8, pl.ds(t, 1), :] = jnp.sum(grad_mixed.astype(F32) * gated, axis=0, keepdims=True)
        xs[9, pl.ds(t, 1), :] = jnp.sum(cot * summed * inverse, axis=0, keepdims=True)
        return carry

    lax.fori_loop(0, tiles, grads, 0)
    gqs_copy.start()
    gm_far.start()
    for copy in gm_copies:
        copy.start()

    def correlate(t, carry):
        grad_mixed = gmx[t, pl.ds(0, K), :]
        source = gext[t]
        group = iota((K, 128), 1) // GS
        left = jnp.concatenate(
            [jnp.where(group == g, grad_mixed, jnp.zeros_like(grad_mixed)) for g in range(per)], axis=0
        )
        cross = lax.dot_general(
            left, source, (((1,), (1,)), ((), ())), preferred_element_type=F32
        )
        for g in range(per):
            block = cross[g * K : (g + 1) * K]
            band = block[:, :K] * mats[0] + block[:, K:] * mats[1]
            folded = band[0:8]
            for a in range(1, K // 8):
                folded = folded + pltpu.roll(band[a * 8 : (a + 1) * 8], K - a * 8, 1)
            glong_s[pl.ds(pl.multiple_of(t * per * 8, 8) + g * 8, 8), :] = folded
        return carry

    lax.fori_loop(0, tiles, correlate, 0)
    folded = glong_s[pl.ds(0, groups, stride=8), :]
    for b in range(1, 8):
        folded = folded + pltpu.roll(glong_s[pl.ds(b, groups, stride=8), :], K - b, 1)
    turned = jnp.dot(folded, flip, precision=HIGH, preferred_element_type=F32)
    for t in range(tiles):
        xs[t] = turned[t * per : (t + 1) * per]
    for i in range(10, INNER):
        xs[i] = jnp.zeros((8, 128), F32)
    tsum[...] = jnp.zeros_like(tsum)

    def copy_to(src, dst, send, recv, device):
        return pltpu.make_async_remote_copy(
            src_ref=src,
            dst_ref=dst,
            send_sem=send,
            recv_sem=recv,
            device_id={"ctx": device},
            device_id_type=MESH_ID,
        )

    def inner_device(k):
        return hi * INNER + inner_peer(k)

    def outer_device(k):
        return outer_peer(k) * INNER + lo

    def scatter(k):
        return copy_to(xs.at[inner_peer(k)], first.at[lo], s1.at[k], r1.at[lo], inner_device(k))

    def exchange(k):
        return copy_to(second.at[hi], second.at[hi], s2.at[k], r2.at[hi], outer_device(k))

    def gather(k):
        return copy_to(result.at[lo], result.at[lo], s3.at[k], r3.at[lo], inner_device(k))

    def near_sums(k):
        return copy_to(near_s.at[lo], near_s.at[lo], s4.at[k], r4.at[lo], inner_device(k))

    def far_sums(k):
        return copy_to(far_s.at[hi], far_s.at[hi], s5.at[k], r5.at[hi], outer_device(k))

    for k in far_first(INNER):
        scatter(k).start()

    heads_back.wait_recv()

    def gate_next(t, carry):
        for s, buf in enumerate((xk, xv)):
            buf[t, pl.ds(RIM + length, RIM), :] = head_r[s, :, lanes(t)].astype(F32)
        sk[t, pl.ds(length, RIM), :] = short_sum(xk, t, 1, length, RIM, taps_m, RIM + length)
        sv[t, pl.ds(length, RIM), :] = short_sum(xv, t, 2, length, RIM, taps_m, RIM + length)
        return carry

    lax.fori_loop(0, tiles, gate_next, 0)
    gqs_copy.wait_recv()
    gm_far.wait_recv()

    def rounded(value):
        return value.astype(BF16).astype(F32)

    def back(t, carry):
        conv = select(
            jnp.dot(umat[t], gmx[t, pl.ds(0, 2 * K), :], preferred_element_type=F32), K
        )
        extra = select(
            jnp.dot(xmat[t], gmx[t, pl.ds(K, 2 * K), :], preferred_element_type=F32), 8
        )
        skip = skip_ref[:, lanes(t)]
        grad_gated = skip * gmx[t, pl.ds(0, K), :].astype(F32) + conv
        ek[t, pl.ds(0, length), :] = rounded(grad_gated * sv[t, pl.ds(0, length), :])
        ev[t, pl.ds(0, length), :] = rounded(grad_gated * sk[t, pl.ds(0, length), :])
        near = gmx[t, pl.ds(K, HEAD), :].astype(F32)[:RIM]
        grad_gated = skip * near + extra
        ek[t, pl.ds(length, RIM), :] = rounded(grad_gated * sv[t, pl.ds(length, RIM), :])
        ev[t, pl.ds(length, RIM), :] = rounded(grad_gated * sk[t, pl.ds(length, RIM), :])
        eq[t, pl.ds(length, RIM), :] = gqs_r[:, lanes(t)].astype(F32)
        for s, (buf, values) in enumerate(((eq, xq), (ek, xk), (ev, xv))):
            own = values[t, pl.ds(RIM, length), :]
            for j in range(KS):
                moved = buf[t, pl.ds(j, length), :] * taps_m[j, pl.ds(RIM + j, length), :]
                tsum[t, pl.ds(s * 8 + j, 1), :] = jnp.sum(moved * own, axis=0, keepdims=True)
        return carry

    for c in range(CHUNKS):
        gm_copies[c].wait_recv()
        lax.fori_loop(c * each, (c + 1) * each, back, 0)
    spread_sums = jnp.zeros((72, 128), F32)
    for t in range(tiles):
        sums = tsum[t]
        high = sums.astype(BF16).astype(F32)
        middle = (sums - high).astype(BF16).astype(F32)
        parts = jnp.concatenate([high, middle, sums - high - middle], axis=0).astype(BF16)
        spread = flag(row // GS + t * per == col).astype(BF16)
        spread_sums = spread_sums + jnp.dot(parts, spread, preferred_element_type=F32)
    spread_sums = spread_sums[0:24] + spread_sums[24:48] + spread_sums[48:72]
    near_s[lo, pl.ds(0, 8), :] = spread_sums[0:8] + pltpu.roll(spread_sums[8:16], 64, 1)
    near_s[lo, pl.ds(8, 8), :] = spread_sums[16:24]
    for k in far_first(INNER):
        near_sums(k).start()
    sums = xs[lo]
    for k in range(1, INNER):
        slot = inner_peer(INNER - k)
        arrived(r1, first, slot)
        sums = sums + first[slot]
    second[hi] = sums
    for k in far_first(outer):
        exchange(k).start()

    def streams(t, carry):
        for s, (buf, out) in enumerate(((eq, gq_out), (ek, gk_out), (ev, gv_out))):
            result_sum = jnp.zeros((length, 128), F32)
            for j in range(KS):
                moved = buf[t, pl.ds(j, length), :] * taps_m[j, pl.ds(RIM + j, length), :]
                result_sum = result_sum + taps_w[t, pl.ds(s * 8 + j, 1), :] * moved
            out[:, lanes(t)] = result_sum.astype(BF16)
        return carry

    lax.fori_loop(0, tiles, streams, 0)

    for k in range(1, outer):
        arrived(r2, second, outer_peer(outer - k))
    sums = second[0]
    for i in range(1, outer):
        sums = sums + second[i]
    result[lo] = sums
    for k in far_first(INNER):
        gather(k).start()

    for k in range(1, INNER):
        arrived(r4, near_s, inner_peer(INNER - k))
    sums = near_s[0]
    for i in range(1, INNER):
        sums = sums + near_s[i]
    far_s[hi] = sums
    for k in far_first(outer):
        far_sums(k).start()

    for k in range(1, INNER):
        arrived(r3, result, inner_peer(INNER - k))
    for t in range(tiles):
        glong_out[pl.ds(t * per, per), :] = result[t]
    gskip_out[...] = result[8]
    ggain_out[...] = result[9]
    for copy in [tails, tails2, heads_k, heads_v, heads_back, gm_far, gqs_copy] + gated_copies + gm_copies:
        copy.wait_send()
    for k in range(1, tp_count):
        share(k).wait_send()
    for k in range(1, INNER):
        scatter(k).wait_send()
        gather(k).wait_send()
        near_sums(k).wait_send()
    for k in range(1, outer):
        exchange(k).wait_send()

    for k in range(1, outer):
        arrived(r5, far_s, outer_peer(outer - k))
    sums = far_s[0]
    for i in range(1, outer):
        sums = sums + far_s[i]
    gshort_out[0] = sums[:KS, :groups]
    gshort_out[1] = sums[:KS, 64 : 64 + groups]
    gshort_out[2] = sums[8 : 8 + KS, :groups]
    for k in range(1, outer):
        far_sums(k).wait_send()


def finish(*refs):
    half = (len(refs) - 1) // 2
    left = refs[-1]
    copies = [pltpu.make_async_copy(refs[i], refs[half + i], left.at[i]) for i in range(half)]
    for copy in copies:
        copy.start()
    for copy in copies:
        copy.wait()


def shards(
    q_input, k_input, v_input, resid, lengths, short_filter, long_filter, skip, gain, cotangent
):
    length, width = q_input.shape
    tiles = width // 128
    groups = width // GS
    per = 128 // GS
    count = lax.axis_size("ctx")
    tp_count = lax.axis_size("tp")
    outer = count // INNER
    vmem = pl.BlockSpec(memory_space=pltpu.VMEM)
    large = pltpu.VMEM((length, width), BF16)

    def tiled(rows):
        return pltpu.VMEM((tiles, rows, 128), F32)

    dma = pltpu.SemaphoreType.DMA
    outs = pl.pallas_call(
        functools.partial(body, count, tp_count),
        out_shape=(
            large,
            large,
            large,
            large,
            pltpu.VMEM((3, KS, groups), F32),
            pltpu.VMEM((groups, K), F32),
            pltpu.VMEM((tiles, 128), F32),
            pltpu.VMEM((tiles, 128), F32),
        ),
        in_specs=[pl.BlockSpec(memory_space=pltpu.SMEM)] + [vmem] * 3 + [pl.BlockSpec(memory_space=pl.ANY)] * 2 + [vmem] * 4,
        out_specs=(vmem,) * 8,
        scratch_shapes=[
            pltpu.VMEM((3, RIM, width), BF16),
            pltpu.VMEM((3, RIM, width), BF16),
            pltpu.VMEM((2, RIM, width), BF16),
            pltpu.VMEM((HEAD, width), BF16),
            pltpu.VMEM((HEAD, width), BF16),
            pltpu.VMEM((2, RIM, width), BF16),
            pltpu.VMEM((2, RIM, width), BF16),
            pltpu.VMEM((tiles, 2 * K, 128), BF16),
            pltpu.VMEM((tiles, 3 * K, 128), BF16),
            pltpu.VMEM((RIM, width), BF16),
            pltpu.VMEM((RIM, width), BF16),
            tiled(length + 2 * RIM),
            tiled(length + 2 * RIM),
            tiled(length + 2 * RIM),
            tiled(RIM + HEAD),
            tiled(RIM + HEAD),
            tiled(length),
            tiled(length + RIM),
            tiled(length + RIM),
            tiled(length),
            tiled(length),
            tiled(length + RIM),
            tiled(length + RIM),
            tiled(length + RIM),
            pltpu.VMEM((tiles, per * K, 2 * K), BF16),
            pltpu.VMEM((tiles, per * K, 2 * K), BF16),
            pltpu.VMEM((tiles, per * 8, 2 * K), BF16),
            pltpu.VMEM((6, K, 128), F32),
            pltpu.VMEM((2, 8, 128), F32),
            pltpu.VMEM((KS, length + 2 * RIM, 128), F32),
            pltpu.VMEM((KS, HEAD, 128), F32),
            tiled(24),
            pltpu.VMEM((groups, K), F32),
            pltpu.VMEM((groups, K), F32),
            pltpu.VMEM((groups * 8, K), F32),
            pltpu.VMEM((tp_count, 8, 128), F32),
            pltpu.VMEM((INNER, 8, 128), F32),
            pltpu.VMEM((INNER, 8, 128), F32),
            pltpu.VMEM((outer, 8, 128), F32),
            pltpu.VMEM((INNER, 8, 128), F32),
            dma((7 + 2 * CHUNKS,)),
            dma((7 + 2 * CHUNKS,)),
            dma((tp_count,)),
            dma((tp_count,)),
            dma((INNER,)),
            dma((INNER,)),
            dma((outer,)),
            dma((outer,)),
            dma((INNER,)),
            dma((INNER,)),
            pltpu.VMEM((INNER, 16, 128), F32),
            pltpu.VMEM((outer, 16, 128), F32),
            tiled(24),
            dma((INNER,)),
            dma((INNER,)),
            dma((outer,)),
            dma((outer,)),
            pltpu.VMEM((length, width), BF16),
            pltpu.VMEM((length, width), BF16),
            dma((2,)),
        ],
        compiler_params=pltpu.CompilerParams(collective_id=0, has_side_effects=True),
        name="operator",
    )(
        lengths,
        q_input,
        k_input,
        v_input,
        resid,
        cotangent,
        jnp.transpose(short_filter, (0, 2, 1)),
        long_filter,
        skip.reshape(1, width),
        gain.reshape(1, width),
    )
    outs = pl.pallas_call(
        finish,
        out_shape=tuple(jax.ShapeDtypeStruct(out.shape, out.dtype) for out in outs),
        in_specs=[vmem] * 8,
        out_specs=(pl.BlockSpec(memory_space=pl.ANY),) * 8,
        scratch_shapes=[dma((8,))],
        name="finish",
    )(*[pltpu.with_memory_space_constraint(out, pltpu.VMEM) for out in outs])
    return outs[:4] + (
        jnp.transpose(outs[4], (0, 2, 1)),
        outs[5],
        outs[6].reshape(width),
        outs[7].reshape(width),
    )


def solution(mesh):
    rows = P("ctx", "tp")
    return jax.shard_map(
        shards,
        mesh=mesh,
        in_specs=(
            rows,
            rows,
            rows,
            rows,
            P(),
            P(None, "tp", None),
            P("tp", None),
            P("tp"),
            P("tp"),
            rows,
        ),
        out_specs=(rows, rows, rows, rows, P(None, "tp", None), P("tp", None), P("tp"), P("tp")),
        check_vma=False,
    )
```
